128 devices in a mesh: blk: 16 (over z, y), beam: 8 (over x, core).
Axes of the slice: x: 4, y: 4, z: 4, core: 2. Of those that a mesh axis runs over, the one named last changes fastest.
Arguments:
- sky_coefficients: bfloat16 [2, 128, 3, 2, 32, 4096], P(None, None, None, None, 'blk'), may hold values from -6 to 6
- beam_window: bfloat16 [2, 16, 4096], P(None, 'beam'), may hold values from -5 to 5
- legendre: bfloat16 [32, 2, 4096, 256], P('blk'), as said below
- azimuth_modes: int32 [32], P('blk'), may hold values from 0 to 8191, as said below
- orientation: float32 [128, 16, 512], P('beam'), may hold values from -1 to 1
Outputs:
- sky_map: bfloat16 [128, 3, 512, 128], P('beam', None, 'blk')
The draws below stay inside these ranges and needn't reach their ends.
Inputs may be any that keep to these rules, and one draw needn't show every extreme that they name: `azimuth_modes`: distinct values; 0 and 8191 are always among them. legendre[m, p, i, t] is zero wherever 2 * i + p < azimuth_modes[m].
All inputs are finite; a program needn't handle non-finite values.
Results may differ from the reference program's by a relative error of at most 0.0049.
Values may be sent and summed in bfloat16 or wider, within the bound.
No kernel may reach another device: no remote copies, remote signals or barrier semaphores. Data moves between devices by JAX's collectives and lax.ppermute only.
A program may use at most 256 MiB of HBM per device.

```python
import math
import jax
import jax.numpy as jnp
from jax import lax

LMAX = 8192
HALF_L = 4096
BEAMK = 16
NSIM = 128
MMODES = 32
RNORTH = 256
CYCLES = 512
NPHI = 128


def mode_list(key):
    base = jax.random.fold_in(key, 4711)
    first_key, second_key = jax.random.split(base)
    shuffled = jax.random.permutation(first_key, LMAX - 2).astype(jnp.int32)
    values = jnp.concatenate([jnp.array([0, LMAX - 1], jnp.int32), shuffled[:MMODES - 2] + 1])
    order = jax.random.permutation(second_key, MMODES)
    return values[order]


def draw_azimuth_modes(key, part):
    return mode_list(key)


def draw_legendre(key, part):
    modes = mode_list(key)
    noise_key = jax.random.fold_in(key, 913)
    shape = (MMODES, 2, LMAX // 2, RNORTH)
    raw = jax.random.normal(noise_key, shape, jnp.float32)
    degree = 2 * jnp.arange(LMAX // 2, dtype=jnp.int32)[None, :] + jnp.arange(2, dtype=jnp.int32)[:, None]
    alive = degree[None, :, :] >= modes[:, None, None]
    count = (LMAX - modes).astype(jnp.float32)
    scale = 1.0 / jnp.sqrt(count * MMODES * BEAMK)
    return jnp.where(alive[:, :, :, None], raw * scale[:, None, None, None], 0.0).astype(jnp.bfloat16)


def shard_levels(stream_key, dims, cuts, least, high):
    gain = 1.0
    for axis_at, blocks in cuts:
        heights = jax.random.uniform(jax.random.fold_in(jax.random.fold_in(stream_key, 6), axis_at), (blocks,), jnp.float32, least / len(cuts), high / len(cuts))
        gain = gain * jnp.repeat(jnp.exp(heights), dims[axis_at] // blocks).reshape((-1,) + (1,) * (len(dims) - 1 - axis_at))
    return gain


def centred(own_key, extent, deviation, bound, cuts=(), held_as=jnp.bfloat16):
    entries = jax.random.normal(own_key, extent, jnp.float32) * deviation
    if len(cuts) > 0:
        entries = shard_levels(own_key, extent, cuts, -0.22, 0.18) * entries
    return jnp.clip(entries, min=-bound, max=bound).astype(held_as)


def setup_inputs(seed: int = 0) -> dict:
    key_list = jax.random.split(jax.random.key(seed), 6)
    return {
        "sky_coefficients": centred(key_list[0], (2, NSIM, 3, 2, MMODES, HALF_L), 1.0, 6.0, ((4, 16),)),
        "beam_window": centred(key_list[1], (2, BEAMK, HALF_L), 1.0, 5.0, ((1, 8),)),
        "legendre": draw_legendre(jax.random.fold_in(key_list[5], 71), 0),
        "azimuth_modes": draw_azimuth_modes(jax.random.fold_in(key_list[5], 71), 0),
        "orientation": jnp.clip(jax.random.uniform(key_list[4], (NSIM, BEAMK, CYCLES), jnp.float32, -1.0, 1.0) * shard_levels(key_list[4], (NSIM, BEAMK, CYCLES), ((0, 8),), -0.4, 0.0), -1.0, 1.0),
    }


def basis_table(azimuth_modes):
    column = jnp.arange(NPHI, dtype=jnp.int32)
    phase = ((azimuth_modes[:, None] * column[None, :]) % (2 * LMAX)).astype(jnp.float32) * (math.pi / LMAX)
    weight = jnp.where(azimuth_modes == 0, 1.0, 2.0).astype(jnp.float32)[:, None]
    return jnp.stack([weight * jnp.cos(phase), -weight * jnp.sin(phase)])


def reference(sky_coefficients, beam_window, legendre, azimuth_modes, orientation):
    nsims = sky_coefficients.shape[1]
    components = beam_window.shape[1]

    def one_mode(index):
        coef = lax.dynamic_index_in_dim(sky_coefficients, index, 4, keepdims=False)
        table = lax.dynamic_index_in_dim(legendre, index, 0, keepdims=False)
        mode = lax.dynamic_index_in_dim(azimuth_modes, index, 0, keepdims=False)
        weighted = (coef[:, :, :, :, None, :].astype(jnp.float32) * beam_window[:, None, None, None, :, :].astype(jnp.float32)).astype(jnp.bfloat16)
        weighted = weighted.reshape(2, -1, HALF_L)
        parts = lax.dot_general(table.astype(jnp.float32), weighted.astype(jnp.float32), (((1,), (2,)), ((0,), (0,))), precision=lax.Precision.HIGHEST, preferred_element_type=jnp.float32)
        sign = jnp.where(mode % 2 == 0, 1.0, -1.0).astype(jnp.float32)
        north = parts[0] + parts[1]
        south = sign * (parts[0] - parts[1])
        cycles = jnp.concatenate([north, jnp.flip(south, 0)], 0)
        cycles = cycles.reshape(2 * RNORTH, nsims, 3, 2, components)
        return jnp.einsum('tscrk,skt->scrt', cycles, orientation, precision=lax.Precision.HIGHEST)

    oriented = lax.map(one_mode, jnp.arange(MMODES, dtype=jnp.int32))
    basis = basis_table(azimuth_modes)
    result = jnp.einsum('mscrt,rmj->sctj', oriented, basis, precision=lax.Precision.HIGHEST)
    return result.astype(jnp.bfloat16)
```

```python
import functools
import math

import jax
import jax.numpy as jnp
from jax import lax
from jax.experimental import pallas as pl
from jax.experimental.pallas import tpu as pltpu
from jax.sharding import PartitionSpec as P

LMAX = 8192
NPHI = 128
CHUNK = 512
BF = jnp.bfloat16
F32 = jnp.float32


def synth_kernel(modes, coef, window, table, weights, out, leg, acc, lhs, win32, sems):
    rows, half = coef.shape[2], coef.shape[3]
    chunks = half // CHUNK
    comps = 2 * window.shape[0]

    def first(slot, p):
        return jnp.minimum((modes[slot] - p + 1) // 2 // CHUNK, chunks - 1)

    def copy(slot, p, c):
        at = pl.ds(pl.multiple_of(c * CHUNK, CHUNK), CHUNK)
        return pltpu.make_async_copy(table.at[slot, p, at, :], leg.at[slot, p, at, :], sems.at[slot, p, c])

    for slot in range(2):
        for p in range(2):
            lax.fori_loop(first(slot, p), chunks, lambda c, _: (copy(slot, p, c).start(), 0)[1], 0)

    for src in range(window.shape[0]):
        for p in range(2):
            win32[p, pl.ds(2 * src, 2), :] = window[src, p].astype(F32)

    def step(slot, p, c):
        copy(slot, p, c).wait()
        at = pl.ds(pl.multiple_of(c * CHUNK, CHUNK), CHUNK)
        sky = coef[slot, p, :, at]
        for k in range(comps):
            gain = jnp.broadcast_to(win32[p, pl.ds(k, 1), at], (rows, CHUNK)).astype(BF)
            lhs[pl.ds(k * rows, rows), :] = sky * gain
        return jnp.dot(lhs[...], leg[slot, p, at, :], preferred_element_type=F32)

    lane = lax.broadcasted_iota(jnp.int32, (256, 256), 0)
    flip = jnp.where(lane + lax.broadcasted_iota(jnp.int32, (256, 256), 1) == 255, 1.0, 0.0).astype(BF)
    group = lax.broadcasted_iota(jnp.int32, (24, 128), 1) // 32
    for slot in range(2):
        for p in range(2):
            acc[p] = jnp.zeros(acc.shape[1:], F32)

            def body(c, _, slot=slot, p=p):
                acc[p] = acc[p] + step(slot, p, c)
                return 0

            lax.fori_loop(first(slot, p), chunks, body, 0)
        sign = jnp.where(modes[slot] % 2 == 0, 1.0, -1.0).astype(F32)
        north, south = [], []
        for b in range(4):
            for c in range(3):
                row = b * 24 + c * 8
                n = jnp.zeros((8, 256), F32)
                s = jnp.zeros((8, 256), F32)
                for k in range(comps):
                    even = acc[0, pl.ds(k * rows + row, 8), :]
                    odd = acc[1, pl.ds(k * rows + row, 8), :]
                    n = n + (even + odd) * weights[k, b, :, pl.ds(0, 256)]
                    s = s + (even - odd) * weights[k, b, :, pl.ds(256, 256)]
                north.append(n)
                south.append(s * sign)
        north = jnp.concatenate(north, 0)
        south = jnp.dot(jnp.concatenate(south, 0).astype(BF), flip, preferred_element_type=F32)
        for tile in range(4):
            half_map = north if tile < 2 else south
            part = half_map[:, (tile % 2) * 128:(tile % 2) * 128 + 128]
            for g in range(4):
                send = jnp.zeros((24, 128), F32)
                for b in range(4):
                    piece = part[b * 24:(b + 1) * 24]
                    if b != g:
                        piece = pltpu.roll(piece, ((b - g) * 32) % 128, 1)
                    send = jnp.where(group == b, piece, send)
                out[tile * 4 + g, pl.ds(slot * 24, 24), :] = send.astype(BF)
    sub = lax.broadcasted_iota(jnp.int32, (8, 128), 0)
    tail = jnp.zeros((8, 128), jnp.int32)
    for slot in range(2):
        tail = jnp.where(sub == 2 * slot, modes[slot] // 128, tail)
        tail = jnp.where(sub == 2 * slot + 1, modes[slot] % 128, tail)
    tail = tail.astype(F32).astype(BF)
    for dst in range(16):
        out[dst, pl.ds(48, 8), :] = tail


def synth(modes, coef, window, table, weights):
    half = coef.shape[3]
    rows = 2 * window.shape[0] * coef.shape[2]
    vm = pl.BlockSpec(memory_space=pltpu.VMEM)
    return pl.pallas_call(
        synth_kernel,
        out_shape=jax.ShapeDtypeStruct((16, 56, 128), BF),
        in_specs=[pl.BlockSpec(memory_space=pltpu.SMEM), vm, vm, pl.BlockSpec(memory_space=pl.ANY), vm],
        out_specs=vm,
        scratch_shapes=[
            pltpu.VMEM((2, 2, half, 256), BF),
            pltpu.VMEM((2, rows, 256), F32),
            pltpu.VMEM((rows, CHUNK), BF),
            pltpu.VMEM((2, 2 * window.shape[0], half), F32),
            pltpu.SemaphoreType.DMA((2, 2, half // CHUNK)),
        ],
        name="synth",
    )(modes, coef, window, table, weights)


def map_kernel(got, out, wide):
    wide[...] = got[...].reshape(wide.shape).astype(F32)

    def take(row):
        return wide[pl.ds(row, 16, stride=56), :]

    column = lax.broadcasted_iota(jnp.int32, (16, 128), 1)
    cosines, sines = [], []
    for slot in range(2):
        mode = (take(48 + 2 * slot) * 128.0 + take(49 + 2 * slot)).astype(jnp.int32)
        phase = ((mode * column) % (2 * LMAX)).astype(F32) * (math.pi / LMAX)
        weight = jnp.where(mode == 0, 1.0, 2.0)
        cosines.append(weight * jnp.cos(phase))
        sines.append(-weight * jnp.sin(phase))
    basis = jnp.concatenate(cosines + sines, 0)
    high = basis.astype(BF)
    low = (basis - high.astype(F32)).astype(BF)
    basis = jnp.concatenate([high, low], 0)
    for c in range(3):
        for a in range(4):
            x = jnp.concatenate([take(slot * 24 + c * 8 + r * 4 + a) for r in range(2) for slot in range(2)], 0)
            x = x.T.astype(BF)
            y = jnp.dot(jnp.concatenate([x, x], 1), basis, preferred_element_type=F32)
            for b in range(4):
                out[4 * a + b, c] = y[b * 32:(b + 1) * 32].astype(BF)


def to_map(got):
    vm = pl.BlockSpec(memory_space=pltpu.VMEM)
    return pl.pallas_call(
        map_kernel,
        out_shape=jax.ShapeDtypeStruct((16, 3, 32, NPHI), BF),
        in_specs=[vm],
        out_specs=vm,
        scratch_shapes=[pltpu.VMEM((16 * 56, 128), F32)],
        name="to_map",
    )(got)


def shards(sky_coefficients, beam_window, legendre, azimuth_modes, orientation):
    half = sky_coefficients.shape[5]
    me = lax.axis_index("beam")
    window = lax.all_to_all(
        jnp.broadcast_to(beam_window[None], (8,) + beam_window.shape), "beam", 0, 0, tiled=True
    )
    coef = lax.dynamic_slice_in_dim(sky_coefficients, me * 16, 16, 1)
    coef = coef.reshape(2, 4, 4, 3, 2, 2, half).transpose(5, 0, 2, 3, 4, 1, 6).reshape(2, 2, 96, half)
    weights = orientation.transpose(1, 0, 2).reshape(16, 4, 1, 4, 512).transpose(0, 3, 2, 1, 4)
    weights = jnp.concatenate([weights[..., :256], jnp.flip(weights[..., 256:], -1)], -1)
    weights = jnp.broadcast_to(weights, (16, 4, 2, 4, 512)).reshape(16, 4, 8, 512)
    sent = synth(azimuth_modes, coef, window, legendre, weights)
    got = lax.all_to_all(sent, "blk", 0, 0, tiled=True)
    return to_map(got)


def solution(mesh):
    placed = (
        P(None, None, None, None, "blk", None),
        P(None, "beam", None),
        P("blk", None, None, None),
        P("blk"),
        P("beam", None, None),
    )
    return jax.shard_map(
        shards, mesh=mesh, in_specs=placed, out_specs=P("beam", None, "blk", None), check_vma=False
    )
```

```python
import math

import jax
import jax.numpy as jnp
from jax import lax
from jax.experimental import pallas as pl
from jax.experimental.pallas import tpu as pltpu
from jax.sharding import PartitionSpec as P

LMAX = 8192
NPHI = 128
CHUNK = 1024
TILES = CHUNK // 128
BLOCK = 16
BF = jnp.bfloat16
F32 = jnp.float32


def mirror():
    lane = lax.broadcasted_iota(jnp.int32, (256, 256), 0)
    return jnp.where(lane + lax.broadcasted_iota(jnp.int32, (256, 256), 1) == 255, 1.0, 0.0).astype(BF)


def arrange_kernel(me, sky, orient, coef, weights, wide, lines):
    del me
    wide[...] = sky[...].astype(F32).reshape(wide.shape)
    for cr in range(6):
        for row in range(BLOCK):
            line = wide[pl.ds(cr * BLOCK + row, 16, stride=6 * BLOCK), :].astype(BF)
            coef[row % 2, 0, pl.ds(cr * 16, 16), pl.ds(row // 2 * 128, 128)] = line

    @pl.when((pl.program_id(0) == 0) & (pl.program_id(1) == 0))
    def _():
        flip = mirror()
        for t in range(4):
            lines[pl.ds(256 * t, 256), :] = orient[:, pl.ds(128 * t, 128)]

        def pick(k, t):
            return lines[pl.ds(256 * t + k, 16, stride=16), :]

        for k in range(16):
            weights[k, :, pl.ds(0, 256)] = jnp.concatenate([pick(k, 0), pick(k, 1)], 1)
        south = jnp.concatenate([jnp.concatenate([pick(k, 2), pick(k, 3)], 1) for k in range(16)], 0)
        total = jnp.zeros((256, 256), F32)
        for _ in range(3):
            piece = south.astype(BF)
            total = total + jnp.dot(piece, flip, preferred_element_type=F32)
            south = south - piece.astype(F32)
        weights[:, :, pl.ds(256, 256)] = total.reshape(16, 16, 256)


def arrange(me, sky, orient):
    half = sky.shape[4] // 2 * 128
    steps = sky.shape[4] // BLOCK
    lanes = BLOCK // 2 * 128
    return pl.pallas_call(
        arrange_kernel,
        out_shape=(
            jax.ShapeDtypeStruct((2, 2, 96, half), BF),
            jax.ShapeDtypeStruct((16, 16, 512), F32),
        ),
        grid_spec=pltpu.PrefetchScalarGridSpec(
            num_scalar_prefetch=1,
            grid=(2, steps),
            in_specs=[
                pl.BlockSpec((1, 16, 3, 2, BLOCK, 128), lambda p, i, me: (p, me[0], 0, 0, i, 0)),
                pl.BlockSpec((256, 512), lambda p, i, me: (0, 0)),
            ],
            out_specs=[
                pl.BlockSpec((2, 1, 96, lanes), lambda p, i, me: (0, p, 0, i)),
                pl.BlockSpec((16, 16, 512), lambda p, i, me: (0, 0, 0)),
            ],
            scratch_shapes=[pltpu.VMEM((96 * BLOCK, 128), F32), pltpu.VMEM((1024, 128), F32)],
        ),
        cost_estimate=pl.CostEstimate(flops=10**8, bytes_accessed=8 * 10**6, transcendentals=0),
        name="arrange",
    )(me, sky, orient)


def synth_kernel(modes, coef, window, table, weights, out, sky, leg, acc, win, sems, coef_sems):
    half = leg.shape[2]
    chunks = half // CHUNK

    def first(slot, p):
        return jnp.minimum((modes[slot] - p + 1) // 2 // CHUNK, chunks - 1)

    def place(c):
        return pl.ds(pl.multiple_of(c * CHUNK, CHUNK), CHUNK)

    def copies(slot, p, c):
        at = place(c)
        return (
            pltpu.make_async_copy(coef.at[slot, p, :, at], sky.at[slot, p, :, at], coef_sems.at[slot, p, c]),
            pltpu.make_async_copy(table.at[slot, p, at, :], leg.at[slot, p, at, :], sems.at[slot, p, c]),
        )

    def begin(slot, p, c):
        for copy in copies(slot, p, c):
            copy.start()

    def finish(slot, p, c):
        for copy in copies(slot, p, c):
            copy.wait()

    for slot in range(2):
        for p in range(2):
            lax.fori_loop(first(slot, p), chunks, lambda c, _: (begin(slot, p, c), 0)[1], 0)

    win[...] = window[...].astype(F32).reshape(win.shape)

    def step(slot, p, c):
        finish(slot, p, c)
        at = place(c)
        lines = [sky[slot, p, pl.ds(16 * j, 16), at] for j in range(6)]
        parts = []
        for k in range(16):
            base = (k // 2 * 2 + p) * (half // 64) + k % 2 + c * (2 * TILES)
            gain = jnp.concatenate(
                [jnp.broadcast_to(win[pl.ds(base + 2 * i, 1), :], (16, 128)).astype(BF) for i in range(TILES)], 1
            )
            parts += [line * gain for line in lines]
        return jnp.dot(jnp.concatenate(parts, 0), leg[slot, p, at, :], preferred_element_type=F32)

    flip = mirror()
    to_row = lax.broadcasted_iota(jnp.int32, (96, 96), 0)
    from_row = lax.broadcasted_iota(jnp.int32, (96, 96), 1)
    wanted = to_row % 24 // 4 * 16 + to_row % 4 * 4 + to_row // 24
    order = jnp.where(from_row == wanted, 1.0, 0.0).astype(BF)
    group = lax.broadcasted_iota(jnp.int32, (24, 128), 1) // 32
    for slot in range(2):
        for p in range(2):
            acc[p] = jnp.zeros(acc.shape[1:], F32)

            def body(c, _, slot=slot, p=p):
                part = step(slot, p, c)
                acc[p] = acc[p] + part
                return 0

            lax.fori_loop(first(slot, p), chunks, body, 0)
        sign = jnp.where(modes[slot] % 2 == 0, 1.0, -1.0).astype(F32)
        north, south = [], []
        for cr in range(6):
            for h in range(2):
                n = jnp.zeros((8, 256), F32)
                s = jnp.zeros((8, 256), F32)
                for k in range(16):
                    at = pl.ds(k * 96 + cr * 16 + h * 8, 8)
                    even, odd = acc[0, at, :], acc[1, at, :]
                    n = n + (even + odd) * weights[k, pl.ds(h * 8, 8), pl.ds(0, 256)]
                    s = s + (even - odd) * weights[k, pl.ds(h * 8, 8), pl.ds(256, 256)]
                north.append(n)
                south.append(s * sign)
        north = jnp.concatenate(north, 0).astype(BF)
        south = jnp.dot(jnp.concatenate(south, 0).astype(BF), flip, preferred_element_type=F32).astype(BF)
        both = jnp.dot(order, jnp.concatenate([north, south], 1), preferred_element_type=F32)
        for tile in range(4):
            part = both[:, tile * 128:(tile + 1) * 128]
            for g in range(4):
                send = jnp.zeros((24, 128), F32)
                for b in range(4):
                    piece = part[b * 24:(b + 1) * 24]
                    if b != g:
                        piece = pltpu.roll(piece, ((b - g) * 32) % 128, 1)
                    send = jnp.where(group == b, piece, send)
                out[tile * 4 + g, pl.ds(slot * 24, 24), :] = send.astype(BF)
    sub = lax.broadcasted_iota(jnp.int32, (8, 128), 0)
    tail = jnp.zeros((8, 128), jnp.int32)
    for slot in range(2):
        tail = jnp.where(sub == 2 * slot, modes[slot] // 128, tail)
        tail = jnp.where(sub == 2 * slot + 1, modes[slot] % 128, tail)
    tail = tail.astype(F32).astype(BF)
    for dst in range(16):
        out[dst, pl.ds(48, 8), :] = tail


def synth(modes, coef, window, table, weights):
    half = coef.shape[3]
    chunks = half // CHUNK
    vm = pl.BlockSpec(memory_space=pltpu.VMEM)
    hbm = pl.BlockSpec(memory_space=pl.ANY)
    return pl.pallas_call(
        synth_kernel,
        out_shape=jax.ShapeDtypeStruct((16, 56, 128), BF),
        in_specs=[pl.BlockSpec(memory_space=pltpu.SMEM), hbm, vm, hbm, vm],
        out_specs=vm,
        scratch_shapes=[
            pltpu.VMEM((2, 2, 96, half), BF),
            pltpu.VMEM((2, 2, half, 256), BF),
            pltpu.VMEM((2, 1536, 256), F32),
            pltpu.VMEM((window.shape[0] * 2 * half // 64, 128), F32),
            pltpu.SemaphoreType.DMA((2, 2, chunks)),
            pltpu.SemaphoreType.DMA((2, 2, chunks)),
        ],
        cost_estimate=pl.CostEstimate(flops=13 * 10**9, bytes_accessed=12 * 10**6, transcendentals=0),
        name="synth",
    )(modes, coef, window, table, weights)


def map_kernel(got, out, wide):
    wide[...] = got[...].reshape(wide.shape).astype(F32)

    def take(row):
        return wide[pl.ds(row, 16, stride=56), :]

    column = lax.broadcasted_iota(jnp.int32, (16, 128), 1)
    cosines, sines = [], []
    for slot in range(2):
        mode = (take(48 + 2 * slot) * 128.0 + take(49 + 2 * slot)).astype(jnp.int32)
        phase = ((mode * column) % (2 * LMAX)).astype(F32) * (math.pi / LMAX)
        weight = jnp.where(mode == 0, 1.0, 2.0)
        cosines.append(weight * jnp.cos(phase))
        sines.append(-weight * jnp.sin(phase))
    basis = jnp.concatenate(cosines + sines, 0)
    high = basis.astype(BF)
    low = (basis - high.astype(F32)).astype(BF)
    basis = jnp.concatenate([high, low], 0)
    for c in range(3):
        for a in range(4):
            x = jnp.concatenate([take(slot * 24 + c * 8 + r * 4 + a) for r in range(2) for slot in range(2)], 0)
            x = x.T.astype(BF)
            y = jnp.dot(jnp.concatenate([x, x], 1), basis, preferred_element_type=F32)
            for b in range(4):
                out[4 * a + b, c] = y[b * 32:(b + 1) * 32].astype(BF)


def to_map(got):
    vm = pl.BlockSpec(memory_space=pltpu.VMEM)
    return pl.pallas_call(
        map_kernel,
        out_shape=jax.ShapeDtypeStruct((16, 3, 32, NPHI), BF),
        in_specs=[vm],
        out_specs=vm,
        scratch_shapes=[pltpu.VMEM((16 * 56, 128), F32)],
        name="to_map",
    )(got)


def paired(x):
    lead = x.shape[:-2]
    x = x.reshape(lead + (2, x.shape[-1] // 128, 128))
    return jnp.swapaxes(x, -3, -2).reshape(lead + (-1, 128))


def shards(sky_coefficients, beam_window, legendre, azimuth_modes, orientation):
    me = lax.axis_index("beam").astype(jnp.int32)[None]
    window = paired(beam_window)
    window = lax.all_to_all(jnp.broadcast_to(window[None], (8,) + window.shape), "beam", 0, 0, tiled=True)
    coef, weights = arrange(me, paired(sky_coefficients), orientation.reshape(256, 512))
    sent = synth(azimuth_modes, coef, window, legendre, weights)
    got = lax.all_to_all(sent, "blk", 0, 0, tiled=True)
    return to_map(got)


def solution(mesh):
    placed = (
        P(None, None, None, None, "blk", None),
        P(None, "beam", None),
        P("blk", None, None, None),
        P("blk"),
        P("beam", None, None),
    )
    return jax.shard_map(
        shards, mesh=mesh, in_specs=placed, out_specs=P("beam", None, "blk", None), check_vma=False
    )
```

```python
import math

import jax
import jax.numpy as jnp
from jax import lax
from jax.experimental import pallas as pl
from jax.experimental.pallas import tpu as pltpu
from jax.sharding import PartitionSpec as P

LMAX = 8192
NPHI = 128
CHUNK = 1024
TILES = CHUNK // 128
BF = jnp.bfloat16
F32 = jnp.float32


def mirror():
    lane = lax.broadcasted_iota(jnp.int32, (256, 256), 0)
    return jnp.where(lane + lax.broadcasted_iota(jnp.int32, (256, 256), 1) == 255, 1.0, 0.0).astype(BF)


def chunk_at(c):
    return pl.ds(pl.multiple_of(c * CHUNK, CHUNK), CHUNK)


def first_chunk(modes, slot, p, chunks):
    return jnp.minimum((modes[slot] - p + 1) // 2 // CHUNK, chunks - 1)


def weighted(lines, win, bases):
    parts = []
    for base in bases:
        gain = [jnp.broadcast_to(win[pl.ds(base + 2 * i, 1), :], (16, 128)).astype(BF) for i in range(TILES)]
        gain = jnp.concatenate(gain, 1)
        parts += [line * gain for line in lines]
    return jnp.concatenate(parts, 0)


def sky_lines(coef, slot, p, c):
    its = [pl.multiple_of(c * TILES, TILES) + i for i in range(TILES)]
    return [
        jnp.concatenate([coef[slot, p, j // 2, it, pl.ds(j % 2 * 16, 16), :] for it in its], 1) for j in range(6)
    ]


def orient_into(start, sums, spins, acc, components):
    for h in range(2):
        n = [None if start is None else start[0, pl.ds(cr * 16 + h * 8, 8), :] for cr in range(6)]
        s = [None if start is None else start[1, pl.ds(cr * 16 + h * 8, 8), :] for cr in range(6)]
        for at, k in enumerate(components):
            spin = spins[k, pl.ds(h * 8, 8), :]
            for cr in range(6):
                rows = pl.ds(at * 96 + cr * 16 + h * 8, 8)
                even, odd = acc[0, rows, :], acc[1, rows, :]
                north = (even + odd) * spin[:, :256]
                south = (even - odd) * spin[:, 256:]
                n[cr] = north if n[cr] is None else n[cr] + north
                s[cr] = south if s[cr] is None else s[cr] + south
        for cr in range(6):
            sums[0, pl.ds(cr * 16 + h * 8, 8), :] = n[cr]
            sums[1, pl.ds(cr * 16 + h * 8, 8), :] = s[cr]


def spread_kernel(window, out, held, sem):
    fetch = pltpu.make_async_copy(window, held, sem)
    fetch.start()
    fetch.wait()
    for dst in range(out.shape[0]):
        out[dst] = held[...]


def spread(window, count):
    return pl.pallas_call(
        spread_kernel,
        out_shape=jax.ShapeDtypeStruct((count,) + window.shape, window.dtype),
        in_specs=[pl.BlockSpec(memory_space=pltpu.HBM)],
        out_specs=pl.BlockSpec(memory_space=pltpu.VMEM),
        scratch_shapes=[pltpu.VMEM(window.shape, window.dtype), pltpu.SemaphoreType.DMA],
        compiler_params=pltpu.CompilerParams(vmem_limit_bytes=2 * 2**20),
        name="spread",
    )(window)


def begin_kernel(
    me, modes_in, sky, orient_in, window, table, coef_out, weights, tail, partial,
    modes, raw, orient, own, win, leg, acc, wide, lines, coef, sems, leg_sems, sky_sems, coef_sems,
):
    mine = me[0]
    chunks = table.shape[2] // CHUNK
    rows = sky.shape[4]
    pitch = 2 * rows + 4
    fetch_modes = pltpu.make_async_copy(modes_in, modes, sems.at[0])
    fetch_orient = pltpu.make_async_copy(orient_in, orient, sems.at[1])
    fetch_window = pltpu.make_async_copy(window, own, sems.at[2])
    fetch_modes.start()

    def sky_copy(p, c):
        return pltpu.make_async_copy(sky.at[p, pl.ds(mine * 16, 16), c], raw.at[p, c], sky_sems.at[p, c])

    fetch_orient.start()
    for p in range(2):
        for c in range(3):
            sky_copy(p, c).start()
    fetch_window.start()
    fetch_modes.wait()

    def leg_copy(slot, p, c):
        at = chunk_at(c)
        return pltpu.make_async_copy(table.at[slot, p, at, :], leg.at[slot, p, at, :], leg_sems.at[slot, p, c])

    for slot in range(2):
        for p in range(2):
            lax.fori_loop(
                first_chunk(modes, slot, p, chunks), chunks, lambda c, _: (leg_copy(slot, p, c).start(), 0)[1], 0
            )

    row = lax.broadcasted_iota(jnp.int32, (8, 128), 0)
    mode = jnp.where(row < 4, modes[0], modes[1])
    column = lax.broadcasted_iota(jnp.int32, (8, 128), 1)
    phase = ((mode * column) % (2 * LMAX)).astype(F32) * (math.pi / LMAX)
    weight = jnp.where(mode == 0, 1.0, 2.0)
    basis = jnp.where(row % 4 < 2, weight * jnp.cos(phase), -weight * jnp.sin(phase))
    high = basis.astype(BF).astype(F32)
    tail[...] = jnp.where(row % 2 == 0, high, basis - high).astype(BF)

    fetch_orient.wait()
    flip = mirror()
    for t in range(4):
        lines[pl.ds(260 * t, 256), :] = orient[:, pl.ds(128 * t, 128)]

    def pick(k, t):
        return lines[pl.ds(260 * t + k, 16, stride=16), :]

    for k in range(16):
        weights[k, :, pl.ds(0, 256)] = jnp.concatenate([pick(k, 0), pick(k, 1)], 1)
    south = jnp.concatenate([jnp.concatenate([pick(k, 2), pick(k, 3)], 1) for k in range(16)], 0)
    total = jnp.zeros((256, 256), F32)
    for _ in range(3):
        piece = south.astype(BF)
        total = total + jnp.dot(piece, flip, preferred_element_type=F32)
        south = south - piece.astype(F32)
    weights[:, :, pl.ds(256, 256)] = total.reshape(16, 16, 256)

    def coef_copy(m, p, c):
        return pltpu.make_async_copy(coef.at[m, p, c], coef_out.at[m, p, c], coef_sems.at[m, p, c])

    def arrange(p, c):
        sky_copy(p, c).wait()
        for s in range(16):
            wide[pl.ds(s * pitch, 2 * rows), :] = raw[p, c, s].reshape(2 * rows, 128).astype(F32)
        for r in range(2):
            for row in range(rows):
                line = wide[pl.ds(r * rows + row, 16, stride=pitch), :].astype(BF)
                coef[row % 2, p, c, row // 2, pl.ds(r * 16, 16), :] = line
        for m in range(2):
            coef_copy(m, p, c).start()

    for p in range(2):
        for c in range(3):
            arrange(p, c)

    fetch_window.wait()
    win[...] = own[...].astype(F32).reshape(win.shape)
    for slot in range(2):
        for p in range(2):

            def body(c, _, slot=slot, p=p):
                leg_copy(slot, p, c).wait()
                base = p * (2 * TILES * chunks) + c * (2 * TILES)
                lhs = weighted(sky_lines(coef, slot, p, c), win, [base, base + 1])
                part = jnp.dot(lhs, leg[slot, p, chunk_at(c), :], preferred_element_type=F32)
                acc[p] = jnp.where(c == first_chunk(modes, slot, p, chunks), 0.0, acc[p]) + part
                return 0

            lax.fori_loop(first_chunk(modes, slot, p, chunks), chunks, body, 0)
        orient_into(None, partial.at[slot], weights, acc, [2 * mine, 2 * mine + 1])
    for m in range(2):
        for p in range(2):
            for c in range(3):
                coef_copy(m, p, c).wait()


def begin(me, modes, sky, orient, window, table):
    half = table.shape[2]
    tiles = half // 128
    vm = pl.BlockSpec(memory_space=pltpu.VMEM)
    hbm = pl.BlockSpec(memory_space=pltpu.HBM)
    return pl.pallas_call(
        begin_kernel,
        out_shape=(
            pltpu.HBM((2, 2, 3, tiles, 32, 128), BF),
            jax.ShapeDtypeStruct((16, 16, 512), F32),
            jax.ShapeDtypeStruct((8, 128), BF),
            jax.ShapeDtypeStruct((2, 2, 96, 256), F32),
        ),
        in_specs=[pl.BlockSpec(memory_space=pltpu.SMEM), hbm, hbm, hbm, hbm, hbm],
        out_specs=(hbm, vm, vm, vm),
        scratch_shapes=[
            pltpu.SMEM((2,), jnp.int32),
            pltpu.VMEM((2, 3, 16, 2, 2 * tiles, 128), BF),
            pltpu.VMEM((256, 512), F32),
            pltpu.VMEM(window.shape, BF),
            pltpu.VMEM((4 * tiles, 128), F32),
            pltpu.VMEM(table.shape, BF),
            pltpu.VMEM((2, 192, 256), F32),
            pltpu.VMEM((64 * tiles + 64, 128), F32),
            pltpu.VMEM((1040, 128), F32),
            pltpu.VMEM((2, 2, 3, tiles, 32, 128), BF),
            pltpu.SemaphoreType.DMA((3,)),
            pltpu.SemaphoreType.DMA((2, 2, half // CHUNK)),
            pltpu.SemaphoreType.DMA((2, 3)),
            pltpu.SemaphoreType.DMA((2, 2, 3)),
        ],
        compiler_params=pltpu.CompilerParams(vmem_limit_bytes=30 * 2**20),
        cost_estimate=pl.CostEstimate(flops=4 * 10**9, bytes_accessed=16 * 10**6, transcendentals=0),
        name="begin",
    )(me, modes, sky, orient, window, table)


def synth_kernel(
    me, modes, coef_in, window, table, weights, tail, partial, out, coef, leg, acc, win, sums, sems, coef_sems
):
    mine = me[0]
    chunks = table.shape[2] // CHUNK
    others = [(mine + 1 + j) % 8 for j in range(7)]

    def copies(slot, p, c):
        at = chunk_at(c)
        its = pl.ds(pl.multiple_of(c * TILES, TILES), TILES)
        return (
            pltpu.make_async_copy(
                coef_in.at[slot, p, :, its], coef.at[slot, p, :, its], coef_sems.at[slot, p, c]
            ),
            pltpu.make_async_copy(table.at[slot, p, at, :], leg.at[slot, p, at, :], sems.at[slot, p, c]),
        )

    def fetch(slot, p, c):
        for copy in copies(slot, p, c):
            copy.start()

    for slot in range(2):
        for p in range(2):
            lax.fori_loop(
                first_chunk(modes, slot, p, chunks), chunks, lambda c, _: (fetch(slot, p, c), 0)[1], 0
            )
    win[...] = window[...].astype(F32).reshape(win.shape)

    def step(slot, p, c):
        for copy in copies(slot, p, c):
            copy.wait()
        bases = [(src * 2 + p) * (2 * TILES * chunks) + c * (2 * TILES) + kk for src in others for kk in range(2)]
        lhs = weighted(sky_lines(coef, slot, p, c), win, bases)
        return jnp.dot(lhs, leg[slot, p, chunk_at(c), :], preferred_element_type=F32)

    def finish(slot):
        orient_into(
            partial.at[slot], sums, weights, acc.at[slot], [2 * src + kk for src in others for kk in range(2)]
        )
        sign = jnp.where(modes[slot] % 2 == 0, 1.0, -1.0).astype(F32)
        north = sums[0].astype(BF)
        south = jnp.dot((sums[1] * sign).astype(BF), flip, preferred_element_type=F32).astype(BF)
        both = jnp.dot(order, jnp.concatenate([north, south], 1), preferred_element_type=F32)
        for tile in range(4):
            part = both[:, tile * 128:(tile + 1) * 128]
            for g in range(4):
                send = jnp.zeros((24, 128), F32)
                for b in range(4):
                    piece = part[b * 24:(b + 1) * 24]
                    if b != g:
                        piece = pltpu.roll(piece, ((b - g) * 32) % 128, 1)
                    send = jnp.where(group == b, piece, send)
                out[tile * 4 + g, pl.ds(slot * 24, 24), :] = send.astype(BF)

    flip = mirror()
    to_row = lax.broadcasted_iota(jnp.int32, (96, 96), 0)
    from_row = lax.broadcasted_iota(jnp.int32, (96, 96), 1)
    wanted = to_row % 24 // 4 * 16 + to_row % 4 * 4 + to_row // 24
    order = jnp.where(from_row == wanted, 1.0, 0.0).astype(BF)
    group = lax.broadcasted_iota(jnp.int32, (24, 128), 1) // 32
    for dst in range(16):
        out[dst, pl.ds(48, 8), :] = tail[...]
    for slot in range(2):
        for p in range(2):
            start = first_chunk(modes, slot, p, chunks)

            def body(c, _, slot=slot, p=p, start=start):
                part = step(slot, p, c)
                acc[slot, p] = jnp.where(c == start, 0.0, acc[slot, p]) + part
                return 0

            lax.fori_loop(start, chunks, body, 0)
        finish(slot)


def synth(me, modes, coef, window, table, weights, tail, partial):
    half = table.shape[2]
    vm = pl.BlockSpec(memory_space=pltpu.VMEM)
    smem = pl.BlockSpec(memory_space=pltpu.SMEM)
    hbm = pl.BlockSpec(memory_space=pltpu.HBM)
    return pl.pallas_call(
        synth_kernel,
        out_shape=jax.ShapeDtypeStruct((16, 56, 128), BF),
        in_specs=[smem, smem, hbm, vm, hbm, vm, vm, vm],
        out_specs=vm,
        scratch_shapes=[
            pltpu.VMEM(coef.shape, BF),
            pltpu.VMEM(table.shape, BF),
            pltpu.VMEM((2, 2, 1344, 256), F32),
            pltpu.VMEM((window.shape[0] * half // 32, 128), F32),
            pltpu.VMEM((2, 96, 256), F32),
            pltpu.SemaphoreType.DMA((2, 2, half // CHUNK)),
            pltpu.SemaphoreType.DMA((2, 2, half // CHUNK)),
        ],
        compiler_params=pltpu.CompilerParams(vmem_limit_bytes=26 * 2**20),
        cost_estimate=pl.CostEstimate(flops=12 * 10**9, bytes_accessed=12 * 10**6, transcendentals=0),
        name="synth",
    )(me, modes, coef, window, table, weights, tail, partial)


def map_kernel(got, out, wide):
    for src in range(16):
        wide[pl.ds(src * 60, 56), :] = got[src].astype(F32)

    def take(row):
        return wide[pl.ds(row, 16, stride=60), :]

    basis = [take(48 + slot * 4 + r * 2 + part) for part in range(2) for r in range(2) for slot in range(2)]
    basis = jnp.concatenate(basis, 0).astype(BF)
    for c in range(3):
        for a in range(4):
            x = jnp.concatenate([take(slot * 24 + c * 8 + r * 4 + a) for r in range(2) for slot in range(2)], 0)
            x = x.T.astype(BF)
            y = jnp.dot(jnp.concatenate([x, x], 1), basis, preferred_element_type=F32)
            for b in range(4):
                out[4 * a + b, c] = y[b * 32:(b + 1) * 32].astype(BF)


def to_map(got):
    vm = pl.BlockSpec(memory_space=pltpu.VMEM)
    return pl.pallas_call(
        map_kernel,
        out_shape=jax.ShapeDtypeStruct((16, 3, 32, NPHI), BF),
        in_specs=[vm],
        out_specs=vm,
        scratch_shapes=[pltpu.VMEM((16 * 60, 128), F32)],
        compiler_params=pltpu.CompilerParams(vmem_limit_bytes=6 * 2**20),
        name="to_map",
    )(got)


def paired(x):
    lead = x.shape[:-2]
    x = x.reshape(lead + (2, x.shape[-1] // 128, 128))
    return jnp.swapaxes(x, -3, -2).reshape(lead + (-1, 128))


def shards(sky_coefficients, beam_window, legendre, azimuth_modes, orientation):
    me = lax.axis_index("beam").astype(jnp.int32)[None]
    def stay(x):
        return pltpu.with_memory_space_constraint(x, pltpu.HBM)

    own = stay(paired(beam_window))
    legendre = stay(legendre)
    window = lax.all_to_all(spread(own, 8), "beam", 0, 0, tiled=True)
    coef, weights, tail, partial = begin(
        me, stay(azimuth_modes), stay(paired(sky_coefficients)), stay(orientation.reshape(256, 512)), own, legendre
    )
    sent = synth(me, azimuth_modes, stay(coef), window, legendre, weights, tail, partial)
    got = lax.all_to_all(sent, "blk", 0, 0, tiled=True)
    return to_map(got)


def solution(mesh):
    placed = (
        P(None, None, None, None, "blk", None),
        P(None, "beam", None),
        P("blk", None, None, None),
        P("blk"),
        P("beam", None, None),
    )
    return jax.shard_map(
        shards, mesh=mesh, in_specs=placed, out_specs=P("beam", None, "blk", None), check_vma=False
    )
```

```python
import math

import jax
import jax.numpy as jnp
from jax import lax
from jax.experimental import pallas as pl
from jax.experimental.layout import Layout, with_layout_constraint
from jax.experimental.pallas import tpu as pltpu
from jax.sharding import PartitionSpec as P

LMAX = 8192
NPHI = 128
CHUNK = 1024
TILES = CHUNK // 128
BF = jnp.bfloat16
F32 = jnp.float32


def mirror():
    lane = lax.broadcasted_iota(jnp.int32, (256, 256), 0)
    return jnp.where(lane + lax.broadcasted_iota(jnp.int32, (256, 256), 1) == 255, 1.0, 0.0).astype(BF)


def chunk_at(c):
    return pl.ds(pl.multiple_of(c * CHUNK, CHUNK), CHUNK)


def first_chunk(modes, slot, p, chunks):
    return jnp.minimum((modes[slot] - p + 1) // 2 // CHUNK, chunks - 1)


def weighted(lines, win, bases, tiles):
    parts = []
    for base in bases:
        gain = [jnp.broadcast_to(win[pl.ds(base + 2 * i, 1), :], (16, 128)).astype(BF) for i in range(tiles)]
        gain = jnp.concatenate(gain, 1)
        parts += [line * gain for line in lines]
    return jnp.concatenate(parts, 0)


def sky_lines(coef, slot, p, tile, tiles):
    return [
        jnp.concatenate([coef[slot, p, j // 2, tile + i, pl.ds(j % 2 * 16, 16), :] for i in range(tiles)], 1)
        for j in range(6)
    ]


def orient(start, spins, acc, components):
    north, south = [None] * 12, [None] * 12
    for h in range(2):
        n = [None if start is None else start[0, pl.ds(cr * 16 + h * 8, 8), :] for cr in range(6)]
        s = [None if start is None else start[1, pl.ds(cr * 16 + h * 8, 8), :] for cr in range(6)]
        for at, k in enumerate(components):
            spin = spins[k, pl.ds(h * 8, 8), :]
            for cr in range(6):
                rows = pl.ds(at * 96 + cr * 16 + h * 8, 8)
                even, odd = acc[0, rows, :], acc[1, rows, :]
                up = (even + odd) * spin[:, :256]
                down = (even - odd) * spin[:, 256:]
                n[cr] = up if n[cr] is None else n[cr] + up
                s[cr] = down if s[cr] is None else s[cr] + down
        for cr in range(6):
            north[2 * cr + h] = n[cr]
            south[2 * cr + h] = s[cr]
    return jnp.concatenate(north, 0), jnp.concatenate(south, 0)


def begin_kernel(
    me, modes_in, sky, orient_in, window, table, coef_out, weights, tail, partial,
    modes, raw, turns, own, win, leg, acc, wide, lines, coef, sems, leg_sems, sky_sems, coef_sems,
):
    mine = me[0]
    chunks = table.shape[2] // CHUNK
    rows = sky.shape[4]
    pitch = 2 * rows + 4
    fetch_modes = pltpu.make_async_copy(modes_in, modes, sems.at[0])
    fetch_orient = pltpu.make_async_copy(orient_in, turns, sems.at[1])
    fetch_window = pltpu.make_async_copy(window, own, sems.at[2])
    fetch_modes.start()

    def sky_copy(p, c):
        return pltpu.make_async_copy(sky.at[p, pl.ds(mine * 16, 16), c], raw.at[p, c], sky_sems.at[p, c])

    fetch_orient.start()
    for p in range(2):
        for c in range(3):
            sky_copy(p, c).start()
    fetch_window.start()
    fetch_modes.wait()

    def leg_copy(slot, p, c):
        at = chunk_at(c)
        return pltpu.make_async_copy(table.at[slot, p, at, :], leg.at[slot, p, at, :], leg_sems.at[slot, p, c])

    for slot in range(2):
        for p in range(2):
            lax.fori_loop(
                first_chunk(modes, slot, p, chunks), chunks, lambda c, _: (leg_copy(slot, p, c).start(), 0)[1], 0
            )

    row = lax.broadcasted_iota(jnp.int32, (8, 128), 0)
    mode = jnp.where(row < 4, modes[0], modes[1])
    column = lax.broadcasted_iota(jnp.int32, (8, 128), 1)
    phase = ((mode * column) % (2 * LMAX)).astype(F32) * (math.pi / LMAX)
    weight = jnp.where(mode == 0, 1.0, 2.0)
    basis = jnp.where(row % 4 < 2, weight * jnp.cos(phase), -weight * jnp.sin(phase))
    high = basis.astype(BF).astype(F32)
    tail[...] = jnp.where(row % 2 == 0, high, basis - high).astype(BF)

    fetch_orient.wait()
    flip = mirror()
    for t in range(4):
        lines[pl.ds(260 * t, 256), :] = turns[:, pl.ds(128 * t, 128)]

    def pick(k, t):
        return lines[pl.ds(260 * t + k, 16, stride=16), :]

    for k in range(16):
        weights[k, :, pl.ds(0, 256)] = jnp.concatenate([pick(k, 0), pick(k, 1)], 1)
    south = jnp.concatenate([jnp.concatenate([pick(k, 2), pick(k, 3)], 1) for k in range(16)], 0)
    total = jnp.zeros((256, 256), F32)
    for _ in range(3):
        piece = south.astype(BF)
        total = total + jnp.dot(piece, flip, preferred_element_type=F32)
        south = south - piece.astype(F32)
    weights[:, :, pl.ds(256, 256)] = total.reshape(16, 16, 256)

    def coef_copy(m, p, c):
        return pltpu.make_async_copy(coef.at[m, p, c], coef_out.at[m, p, c], coef_sems.at[m, p, c])

    def arrange(p, c):
        sky_copy(p, c).wait()
        for s in range(16):
            wide[pl.ds(s * pitch, 2 * rows), :] = raw[p, c, s].reshape(2 * rows, 128).astype(F32)
        for r in range(2):
            for row in range(rows):
                line = wide[pl.ds(r * rows + row, 16, stride=pitch), :].astype(BF)
                coef[row % 2, p, c, row // 2, pl.ds(r * 16, 16), :] = line
        for m in range(2):
            coef_copy(m, p, c).start()

    for p in range(2):
        for c in range(3):
            arrange(p, c)

    fetch_window.wait()
    win[...] = own[...].astype(F32).reshape(win.shape)
    for slot in range(2):
        for p in range(2):

            def body(c, _, slot=slot, p=p):
                leg_copy(slot, p, c).wait()
                base = p * (2 * TILES * chunks) + c * (2 * TILES)
                tile = pl.multiple_of(c * TILES, TILES)
                lhs = weighted(sky_lines(coef, slot, p, tile, TILES), win, [base, base + 1], TILES)
                part = jnp.dot(lhs, leg[slot, p, chunk_at(c), :], preferred_element_type=F32)
                acc[p] = jnp.where(c == first_chunk(modes, slot, p, chunks), 0.0, acc[p]) + part
                return 0

            lax.fori_loop(first_chunk(modes, slot, p, chunks), chunks, body, 0)
        partial[slot, 0], partial[slot, 1] = orient(None, weights, acc, [2 * mine, 2 * mine + 1])
    for m in range(2):
        for p in range(2):
            for c in range(3):
                coef_copy(m, p, c).wait()


def begin(me, modes, sky, orient, window, table):
    half = table.shape[2]
    tiles = half // 128
    vm = pl.BlockSpec(memory_space=pltpu.VMEM)
    hbm = pl.BlockSpec(memory_space=pltpu.HBM)
    return pl.pallas_call(
        begin_kernel,
        out_shape=(
            pltpu.HBM((2, 2, 3, tiles, 32, 128), BF),
            jax.ShapeDtypeStruct((16, 16, 512), F32),
            jax.ShapeDtypeStruct((8, 128), BF),
            jax.ShapeDtypeStruct((2, 2, 96, 256), F32),
        ),
        in_specs=[pl.BlockSpec(memory_space=pltpu.SMEM), hbm, hbm, hbm, hbm, hbm],
        out_specs=(hbm, vm, vm, vm),
        scratch_shapes=[
            pltpu.SMEM((2,), jnp.int32),
            pltpu.VMEM((2, 3, 16, 2, 2 * tiles, 128), BF),
            pltpu.VMEM((256, 512), F32),
            pltpu.VMEM(window.shape, BF),
            pltpu.VMEM((4 * tiles, 128), F32),
            pltpu.VMEM(table.shape, BF),
            pltpu.VMEM((2, 192, 256), F32),
            pltpu.VMEM((64 * tiles + 64, 128), F32),
            pltpu.VMEM((1040, 128), F32),
            pltpu.VMEM((2, 2, 3, tiles, 32, 128), BF),
            pltpu.SemaphoreType.DMA((3,)),
            pltpu.SemaphoreType.DMA((2, 2, half // CHUNK)),
            pltpu.SemaphoreType.DMA((2, 3)),
            pltpu.SemaphoreType.DMA((2, 2, 3)),
        ],
        compiler_params=pltpu.CompilerParams(vmem_limit_bytes=30 * 2**20),
        cost_estimate=pl.CostEstimate(flops=4 * 10**9, bytes_accessed=16 * 10**6, transcendentals=0),
        name="begin",
    )(me, modes, sky, orient, window, table)


def synth_kernel(
    me, modes, coef_in, window, table, weights, tail, partial, out, coef, leg, acc, win, maps, sems, coef_sems
):
    mine = me[0]
    halves = table.shape[2] // CHUNK * 2
    others = [(mine + 1 + j) % 8 for j in range(7)]

    def span(slot, p):
        count = halves - jnp.minimum((modes[slot] - p + 1) // 2 // (CHUNK // 2), halves - 1)
        return (halves - count + 1) // 2, count % 2 == 1

    def copies(slot, p, c, tile, tiles):
        at = pl.ds(pl.multiple_of(tile * 128, tiles * 128), tiles * 128)
        its = pl.ds(pl.multiple_of(tile, tiles), tiles)
        return (
            pltpu.make_async_copy(
                coef_in.at[slot, p, :, its], coef.at[slot, p, :, its], coef_sems.at[slot, p, c]
            ),
            pltpu.make_async_copy(table.at[slot, p, at, :], leg.at[slot, p, at, :], sems.at[slot, p, c]),
        )

    def whole(c):
        return c, c * TILES, TILES

    def part(c):
        return c - 1, c * TILES - TILES // 2, TILES // 2

    def fetch(slot, p, where):
        for copy in copies(slot, p, *where):
            copy.start()

    for slot in range(2):
        for p in range(2):
            start, half = span(slot, p)

            @pl.when(half)
            def _(slot=slot, p=p, start=start):
                fetch(slot, p, part(start))

            lax.fori_loop(start, halves // 2, lambda c, _: (fetch(slot, p, whole(c)), 0)[1], 0)
    win[...] = window[...].astype(F32).reshape(win.shape)

    def step(slot, p, c, tile, tiles):
        for copy in copies(slot, p, c, tile, tiles):
            copy.wait()
        tile = pl.multiple_of(tile, tiles)
        at = pl.ds(pl.multiple_of(tile * 128, tiles * 128), tiles * 128)
        bases = [(src * 2 + p) * (halves * TILES) + 2 * tile + kk for src in others for kk in range(2)]
        lhs = weighted(sky_lines(coef, slot, p, tile, tiles), win, bases, tiles)
        return jnp.dot(lhs, leg[slot, p, at, :], preferred_element_type=F32)

    for dst in range(16):
        out[dst, pl.ds(48, 8), :] = tail[...]
    for slot in range(2):
        for p in range(2):
            start, half = span(slot, p)

            @pl.when(half)
            def _(slot=slot, p=p, start=start):
                acc[slot, p] = step(slot, p, *part(start))

            fresh = jnp.where(half, -1, start)

            def body(c, _, slot=slot, p=p, fresh=fresh):
                more = step(slot, p, *whole(c))
                acc[slot, p] = jnp.where(c == fresh, 0.0, acc[slot, p]) + more
                return 0

            lax.fori_loop(start, halves // 2, body, 0)

    flip = mirror()
    group = lax.broadcasted_iota(jnp.int32, (24, 128), 1) // 32
    components = [2 * src + kk for src in others for kk in range(2)]
    for slot in range(2):
        sign = jnp.where(modes[slot] % 2 == 0, 1.0, -1.0).astype(F32)
        north, south = orient(partial.at[slot], weights, acc.at[slot], components)
        south = jnp.dot((south * sign).astype(BF), flip, preferred_element_type=F32)
        for tile in range(4):
            hemisphere = north if tile < 2 else south
            maps[slot, tile] = hemisphere[:, tile % 2 * 128:tile % 2 * 128 + 128]
    for slot in range(2):
        for tile in range(4):
            pieces = [maps[slot, tile, pl.ds(b, 24, stride=4), :] for b in range(4)]
            for g in range(4):
                send = pieces[g]
                for b in range(4):
                    if b != g:
                        send = jnp.where(group == b, pltpu.roll(pieces[b], ((b - g) * 32) % 128, 1), send)
                out[tile * 4 + g, pl.ds(slot * 24, 24), :] = send.astype(BF)


def synth(me, modes, coef, window, table, weights, tail, partial):
    half = table.shape[2]
    vm = pl.BlockSpec(memory_space=pltpu.VMEM)
    smem = pl.BlockSpec(memory_space=pltpu.SMEM)
    hbm = pl.BlockSpec(memory_space=pltpu.HBM)
    return pl.pallas_call(
        synth_kernel,
        out_shape=jax.ShapeDtypeStruct((16, 56, 128), BF),
        in_specs=[smem, smem, hbm, vm, hbm, vm, vm, vm],
        out_specs=vm,
        scratch_shapes=[
            pltpu.VMEM(coef.shape, BF),
            pltpu.VMEM(table.shape, BF),
            pltpu.VMEM((2, 2, 1344, 256), F32),
            pltpu.VMEM((window.shape[0] * half // 32, 128), F32),
            pltpu.VMEM((2, 4, 96, 128), F32),
            pltpu.SemaphoreType.DMA((2, 2, half // CHUNK)),
            pltpu.SemaphoreType.DMA((2, 2, half // CHUNK)),
        ],
        compiler_params=pltpu.CompilerParams(vmem_limit_bytes=26 * 2**20),
        cost_estimate=pl.CostEstimate(flops=12 * 10**9, bytes_accessed=12 * 10**6, transcendentals=0),
        name="synth",
    )(me, modes, coef, window, table, weights, tail, partial)


def map_kernel(got, out, wide):
    for src in range(16):
        wide[pl.ds(src * 60, 56), :] = got[src].astype(F32)

    def take(row):
        return wide[pl.ds(row, 16, stride=60), :]

    basis = [take(48 + slot * 4 + r * 2 + part) for part in range(2) for r in range(2) for slot in range(2)]
    basis = jnp.concatenate(basis, 0).astype(BF)
    for c in range(3):
        for a in range(4):
            x = jnp.concatenate([take(slot * 24 + c * 8 + r * 4 + a) for r in range(2) for slot in range(2)], 0)
            x = x.T.astype(BF)
            y = jnp.dot(jnp.concatenate([x, x], 1), basis, preferred_element_type=F32)
            for b in range(4):
                out[4 * a + b, c] = y[b * 32:(b + 1) * 32].astype(BF)


def to_map(got):
    vm = pl.BlockSpec(memory_space=pltpu.VMEM)
    return pl.pallas_call(
        map_kernel,
        out_shape=jax.ShapeDtypeStruct((16, 3, 32, NPHI), BF),
        in_specs=[vm],
        out_specs=vm,
        scratch_shapes=[pltpu.VMEM((16 * 60, 128), F32)],
        compiler_params=pltpu.CompilerParams(vmem_limit_bytes=6 * 2**20),
        name="to_map",
    )(got)


def paired(x):
    lead = x.shape[:-2]
    x = x.reshape(lead + (2, x.shape[-1] // 128, 128))
    return jnp.swapaxes(x, -3, -2).reshape(lead + (-1, 128))


def rowwise(x):
    return with_layout_constraint(x, Layout(major_to_minor=tuple(range(x.ndim))))


def shards(sky_coefficients, beam_window, legendre, azimuth_modes, orientation):
    me = lax.axis_index("beam").astype(jnp.int32)[None]
    def stay(x):
        return pltpu.with_memory_space_constraint(x, pltpu.HBM)

    own = stay(paired(beam_window))
    legendre = stay(legendre)
    window = lax.all_to_all(jnp.broadcast_to(rowwise(paired(beam_window))[None], (8,) + own.shape), "beam", 0, 0, tiled=True)
    coef, weights, tail, partial = begin(
        me, stay(azimuth_modes), stay(paired(sky_coefficients)), stay(orientation.reshape(256, 512)), own, legendre
    )
    sent = synth(me, azimuth_modes, stay(coef), window, legendre, weights, tail, partial)
    got = lax.all_to_all(sent, "blk", 0, 0, tiled=True)
    return to_map(got)


def solution(mesh):
    placed = (
        P(None, None, None, None, "blk", None),
        P(None, "beam", None),
        P("blk", None, None, None),
        P("blk"),
        P("beam", None, None),
    )
    return jax.shard_map(
        shards, mesh=mesh, in_specs=placed, out_specs=P("beam", None, "blk", None), check_vma=False
    )
```

```python
import math

import jax
import jax.numpy as jnp
from jax import lax
from jax.experimental import pallas as pl
from jax.experimental.layout import Layout, with_layout_constraint
from jax.experimental.pallas import tpu as pltpu
from jax.sharding import PartitionSpec as P

LMAX = 8192
NPHI = 128
CHUNK = 1024
TILES = CHUNK // 128
BF = jnp.bfloat16
F32 = jnp.float32


def mirror():
    lane = lax.broadcasted_iota(jnp.int32, (256, 256), 0)
    return jnp.where(lane + lax.broadcasted_iota(jnp.int32, (256, 256), 1) == 255, 1.0, 0.0).astype(BF)


def chunk_at(c):
    return pl.ds(pl.multiple_of(c * CHUNK, CHUNK), CHUNK)


def first_chunk(modes, slot, p, chunks):
    return jnp.minimum((modes[slot] - p + 1) // 2 // CHUNK, chunks - 1)


def weighted(lines, win, bases, tiles):
    parts = []
    for base in bases:
        gain = [jnp.broadcast_to(win[pl.ds(base + 2 * i, 1), :], (16, 128)).astype(BF) for i in range(tiles)]
        gain = jnp.concatenate(gain, 1)
        parts += [line * gain for line in lines]
    return jnp.concatenate(parts, 0)


def sky_lines(coef, slot, p, tile, tiles):
    return [
        jnp.concatenate([coef[slot, p, j // 2, tile + i, pl.ds(j % 2 * 16, 16), :] for i in range(tiles)], 1)
        for j in range(6)
    ]


def orient(start, spins, acc, components):
    north, south = [None] * 12, [None] * 12
    for h in range(2):
        n = [None if start is None else start[0, pl.ds(cr * 16 + h * 8, 8), :] for cr in range(6)]
        s = [None if start is None else start[1, pl.ds(cr * 16 + h * 8, 8), :] for cr in range(6)]
        for at, k in enumerate(components):
            spin = spins[k, pl.ds(h * 8, 8), :]
            for cr in range(6):
                rows = pl.ds(at * 96 + cr * 16 + h * 8, 8)
                even, odd = acc[0, rows, :], acc[1, rows, :]
                up = (even + odd) * spin[:, :256]
                down = (even - odd) * spin[:, 256:]
                n[cr] = up if n[cr] is None else n[cr] + up
                s[cr] = down if s[cr] is None else s[cr] + down
        for cr in range(6):
            north[2 * cr + h] = n[cr]
            south[2 * cr + h] = s[cr]
    return jnp.concatenate(north, 0), jnp.concatenate(south, 0)


def begin_kernel(
    me, modes_in, sky, orient_in, window, table, coef_out, weights, tail, partial, lead_coef, lead_leg,
    modes, raw, turns, own, win, leg, acc, wide, lines, coef, sems, leg_sems, sky_sems, coef_sems, lead_sems,
):
    mine = me[0]
    chunks = table.shape[2] // CHUNK
    rows = sky.shape[4]
    pitch = 2 * rows + 4
    fetch_modes = pltpu.make_async_copy(modes_in, modes, sems.at[0])
    fetch_orient = pltpu.make_async_copy(orient_in, turns, sems.at[1])
    fetch_window = pltpu.make_async_copy(window, own, sems.at[2])
    fetch_modes.start()

    def sky_copy(p, c):
        return pltpu.make_async_copy(sky.at[p, pl.ds(mine * 16, 16), c], raw.at[p, c], sky_sems.at[p, c])

    fetch_orient.start()
    for p in range(2):
        for c in range(3):
            sky_copy(p, c).start()
    fetch_window.start()
    fetch_modes.wait()

    def leg_copy(slot, p, c):
        at = chunk_at(c)
        return pltpu.make_async_copy(table.at[slot, p, at, :], leg.at[slot, p, at, :], leg_sems.at[slot, p, c])

    for slot in range(2):
        for p in range(2):
            lax.fori_loop(
                first_chunk(modes, slot, p, chunks), chunks, lambda c, _: (leg_copy(slot, p, c).start(), 0)[1], 0
            )

    row = lax.broadcasted_iota(jnp.int32, (8, 128), 0)
    mode = jnp.where(row < 4, modes[0], modes[1])
    column = lax.broadcasted_iota(jnp.int32, (8, 128), 1)
    phase = ((mode * column) % (2 * LMAX)).astype(F32) * (math.pi / LMAX)
    weight = jnp.where(mode == 0, 1.0, 2.0)
    basis = jnp.where(row % 4 < 2, weight * jnp.cos(phase), -weight * jnp.sin(phase))
    high = basis.astype(BF).astype(F32)
    tail[...] = jnp.where(row % 2 == 0, high, basis - high).astype(BF)

    fetch_orient.wait()
    flip = mirror()
    for t in range(4):
        for s in range(16):
            lines[pl.ds(320 * t + 20 * s, 16), :] = turns[pl.ds(16 * s, 16), pl.ds(128 * t, 128)]

    def pick(k, t):
        return lines[pl.ds(320 * t + k, 16, stride=20), :]

    for k in range(16):
        weights[k, :, pl.ds(0, 256)] = jnp.concatenate([pick(k, 0), pick(k, 1)], 1)
    south = jnp.concatenate([jnp.concatenate([pick(k, 2), pick(k, 3)], 1) for k in range(16)], 0)
    total = jnp.zeros((256, 256), F32)
    for _ in range(3):
        piece = south.astype(BF)
        total = total + jnp.dot(piece, flip, preferred_element_type=F32)
        south = south - piece.astype(F32)
    weights[:, :, pl.ds(256, 256)] = total.reshape(16, 16, 256)

    def coef_copy(m, p, c):
        return pltpu.make_async_copy(coef.at[m, p, c], coef_out.at[m, p, c], coef_sems.at[m, p, c])

    def arrange(p, c):
        sky_copy(p, c).wait()
        for s in range(16):
            wide[pl.ds(s * pitch, 2 * rows), :] = raw[p, c, s].reshape(2 * rows, 128).astype(F32)
        for r in range(2):
            for row in range(rows):
                line = wide[pl.ds(r * rows + row, 16, stride=pitch), :].astype(BF)
                coef[row % 2, p, c, row // 2, pl.ds(r * 16, 16), :] = line
        for m in range(2):
            coef_copy(m, p, c).start()

    for p in range(2):
        for c in range(3):
            arrange(p, c)

    def lead_copies():
        c = first_chunk(modes, 0, 0, chunks)
        its = pl.ds(pl.multiple_of(c * TILES, TILES), TILES)
        return (
            pltpu.make_async_copy(coef.at[0, 0, :, its], lead_coef, lead_sems.at[0]),
            pltpu.make_async_copy(leg.at[0, 0, chunk_at(c), :], lead_leg, lead_sems.at[1]),
        )

    fetch_window.wait()
    win[...] = own[...].astype(F32).reshape(win.shape)
    for slot in range(2):
        for p in range(2):

            def body(c, _, slot=slot, p=p):
                leg_copy(slot, p, c).wait()
                base = p * (2 * TILES * chunks) + c * (2 * TILES)
                tile = pl.multiple_of(c * TILES, TILES)
                lhs = weighted(sky_lines(coef, slot, p, tile, TILES), win, [base, base + 1], TILES)
                part = jnp.dot(lhs, leg[slot, p, chunk_at(c), :], preferred_element_type=F32)
                acc[p] = jnp.where(c == first_chunk(modes, slot, p, chunks), 0.0, acc[p]) + part
                return 0

            lax.fori_loop(first_chunk(modes, slot, p, chunks), chunks, body, 0)
        if slot == 0:
            for copy in lead_copies():
                copy.start()
        partial[slot, 0], partial[slot, 1] = orient(None, weights, acc, [2 * mine, 2 * mine + 1])
    for copy in lead_copies():
        copy.wait()
    for m in range(2):
        for p in range(2):
            for c in range(3):
                coef_copy(m, p, c).wait()


def begin(me, modes, sky, orient, window, table):
    half = table.shape[2]
    tiles = half // 128
    vm = pl.BlockSpec(memory_space=pltpu.VMEM)
    hbm = pl.BlockSpec(memory_space=pltpu.HBM)
    return pl.pallas_call(
        begin_kernel,
        out_shape=(
            pltpu.HBM((2, 2, 3, tiles, 32, 128), BF),
            jax.ShapeDtypeStruct((16, 16, 512), F32),
            jax.ShapeDtypeStruct((8, 128), BF),
            jax.ShapeDtypeStruct((2, 2, 96, 256), F32),
            jax.ShapeDtypeStruct((3, TILES, 32, 128), BF),
            jax.ShapeDtypeStruct((CHUNK, 256), BF),
        ),
        in_specs=[pl.BlockSpec(memory_space=pltpu.SMEM), hbm, hbm, hbm, hbm, hbm],
        out_specs=(hbm, vm, vm, vm, vm, vm),
        scratch_shapes=[
            pltpu.SMEM((2,), jnp.int32),
            pltpu.VMEM((2, 3, 16, 2, 2 * tiles, 128), BF),
            pltpu.VMEM((256, 512), F32),
            pltpu.VMEM(window.shape, BF),
            pltpu.VMEM((4 * tiles, 128), F32),
            pltpu.VMEM(table.shape, BF),
            pltpu.VMEM((2, 192, 256), F32),
            pltpu.VMEM((64 * tiles + 64, 128), F32),
            pltpu.VMEM((1280, 128), F32),
            pltpu.VMEM((2, 2, 3, tiles, 32, 128), BF),
            pltpu.SemaphoreType.DMA((3,)),
            pltpu.SemaphoreType.DMA((2, 2, half // CHUNK)),
            pltpu.SemaphoreType.DMA((2, 3)),
            pltpu.SemaphoreType.DMA((2, 2, 3)),
            pltpu.SemaphoreType.DMA((2,)),
        ],
        compiler_params=pltpu.CompilerParams(vmem_limit_bytes=30 * 2**20),
        cost_estimate=pl.CostEstimate(flops=4 * 10**9, bytes_accessed=16 * 10**6, transcendentals=0),
        name="begin",
    )(me, modes, sky, orient, window, table)


def synth_kernel(
    me, modes, coef_in, window, table, weights, tail, partial, lead_coef, lead_leg,
    out, coef, leg, acc, win, maps, sems, coef_sems,
):
    mine = me[0]
    halves = table.shape[2] // CHUNK * 2
    others = [(mine + 1 + j) % 8 for j in range(7)]

    def span(slot, p):
        count = halves - jnp.minimum((modes[slot] - p + 1) // 2 // (CHUNK // 2), halves - 1)
        return (halves - count + 1) // 2, count % 2 == 1

    def copies(slot, p, c, tile, tiles):
        at = pl.ds(pl.multiple_of(tile * 128, tiles * 128), tiles * 128)
        its = pl.ds(pl.multiple_of(tile, tiles), tiles)
        return (
            pltpu.make_async_copy(
                coef_in.at[slot, p, :, its], coef.at[slot, p, :, its], coef_sems.at[slot, p, c]
            ),
            pltpu.make_async_copy(table.at[slot, p, at, :], leg.at[slot, p, at, :], sems.at[slot, p, c]),
        )

    def whole(c):
        return c, c * TILES, TILES

    def part(c):
        return c - 1, c * TILES - TILES // 2, TILES // 2

    def fetch(slot, p, where):
        for copy in copies(slot, p, *where):
            copy.start()

    def lead(at, tile, tiles):
        to = pl.ds(pl.multiple_of(tile * 128, tiles * 128), tiles * 128)
        its = pl.ds(pl.multiple_of(tile, tiles), tiles)
        c = tile // TILES
        return (
            pltpu.make_async_copy(lead_coef.at[:, pl.ds(at, tiles)], coef.at[0, 0, :, its], coef_sems.at[0, 0, c]),
            pltpu.make_async_copy(lead_leg.at[pl.ds(at * 128, tiles * 128)], leg.at[0, 0, to, :], sems.at[0, 0, c]),
        )

    def fetch_lead(at, where):
        for copy in lead(at, *where[1:]):
            copy.start()

    for slot in range(2):
        for p in range(2):
            start, half = span(slot, p)
            rest = start
            if slot == 0 and p == 0:

                @pl.when(half)
                def _(start=start):
                    fetch_lead(TILES // 2, part(start))

                @pl.when(jnp.logical_not(half))
                def _(start=start):
                    fetch_lead(0, whole(start))

                rest = jnp.where(half, start, start + 1)
            else:

                @pl.when(half)
                def _(slot=slot, p=p, start=start):
                    fetch(slot, p, part(start))

            lax.fori_loop(rest, halves // 2, lambda c, _: (fetch(slot, p, whole(c)), 0)[1], 0)
    win[...] = window[...].astype(F32).reshape(win.shape)

    def step(slot, p, c, tile, tiles):
        for copy in copies(slot, p, c, tile, tiles):
            copy.wait()
        tile = pl.multiple_of(tile, tiles)
        at = pl.ds(pl.multiple_of(tile * 128, tiles * 128), tiles * 128)
        bases = [(src * 2 + p) * (halves * TILES) + 2 * tile + kk for src in others for kk in range(2)]
        lhs = weighted(sky_lines(coef, slot, p, tile, tiles), win, bases, tiles)
        return jnp.dot(lhs, leg[slot, p, at, :], preferred_element_type=F32)

    for dst in range(16):
        out[dst, pl.ds(48, 8), :] = tail[...]
    for slot in range(2):
        for p in range(2):
            start, half = span(slot, p)

            @pl.when(half)
            def _(slot=slot, p=p, start=start):
                acc[slot, p] = step(slot, p, *part(start))

            fresh = jnp.where(half, -1, start)

            def body(c, _, slot=slot, p=p, fresh=fresh):
                more = step(slot, p, *whole(c))
                acc[slot, p] = jnp.where(c == fresh, 0.0, acc[slot, p]) + more
                return 0

            lax.fori_loop(start, halves // 2, body, 0)

    flip = mirror()
    group = lax.broadcasted_iota(jnp.int32, (24, 128), 1) // 32
    components = [2 * src + kk for src in others for kk in range(2)]
    for slot in range(2):
        sign = jnp.where(modes[slot] % 2 == 0, 1.0, -1.0).astype(F32)
        north, south = orient(partial.at[slot], weights, acc.at[slot], components)
        south = jnp.dot((south * sign).astype(BF), flip, preferred_element_type=F32)
        for tile in range(4):
            hemisphere = north if tile < 2 else south
            maps[slot, tile] = hemisphere[:, tile % 2 * 128:tile % 2 * 128 + 128]
    for slot in range(2):
        for tile in range(4):
            pieces = [maps[slot, tile, pl.ds(b, 24, stride=4), :] for b in range(4)]
            for g in range(4):
                send = pieces[g]
                for b in range(4):
                    if b != g:
                        send = jnp.where(group == b, pltpu.roll(pieces[b], ((b - g) * 32) % 128, 1), send)
                out[tile * 4 + g, pl.ds(slot * 24, 24), :] = send.astype(BF)


def synth(me, modes, coef, window, table, *rest):
    half = table.shape[2]
    vm = pl.BlockSpec(memory_space=pltpu.VMEM)
    smem = pl.BlockSpec(memory_space=pltpu.SMEM)
    hbm = pl.BlockSpec(memory_space=pltpu.HBM)
    return pl.pallas_call(
        synth_kernel,
        out_shape=jax.ShapeDtypeStruct((16, 56, 128), BF),
        in_specs=[smem, smem, hbm, vm, hbm, vm, vm, vm, vm, vm],
        out_specs=vm,
        scratch_shapes=[
            pltpu.VMEM(coef.shape, BF),
            pltpu.VMEM(table.shape, BF),
            pltpu.VMEM((2, 2, 1344, 256), F32),
            pltpu.VMEM((window.shape[0] * half // 32, 128), F32),
            pltpu.VMEM((2, 4, 96, 128), F32),
            pltpu.SemaphoreType.DMA((2, 2, half // CHUNK)),
            pltpu.SemaphoreType.DMA((2, 2, half // CHUNK)),
        ],
        compiler_params=pltpu.CompilerParams(vmem_limit_bytes=26 * 2**20),
        cost_estimate=pl.CostEstimate(flops=12 * 10**9, bytes_accessed=12 * 10**6, transcendentals=0),
        name="synth",
    )(me, modes, coef, window, table, *rest)


def map_kernel(got, out, wide, held, sems):
    for src in range(16):
        wide[pl.ds(src * 60, 56), :] = got[src].astype(F32)

    def take(row):
        return wide[pl.ds(row, 16, stride=60), :]

    basis = [take(48 + slot * 4 + r * 2 + part) for part in range(2) for r in range(2) for slot in range(2)]
    basis = jnp.concatenate(basis, 0).astype(BF)
    for c in range(3):
        for a in range(4):
            x = jnp.concatenate([take(slot * 24 + c * 8 + r * 4 + a) for r in range(2) for slot in range(2)], 0)
            x = x.T.astype(BF)
            y = jnp.dot(jnp.concatenate([x, x], 1), basis, preferred_element_type=F32)
            for b in range(4):
                held[c, 4 * a + b] = y[b * 32:(b + 1) * 32].astype(BF)
        pltpu.make_async_copy(held.at[c], out.at[:, c], sems.at[c]).start()
    for c in range(3):
        pltpu.make_async_copy(held.at[c], out.at[:, c], sems.at[c]).wait()


def to_map(got):
    vm = pl.BlockSpec(memory_space=pltpu.VMEM)
    return pl.pallas_call(
        map_kernel,
        out_shape=pltpu.HBM((16, 3, 32, NPHI), BF),
        in_specs=[vm],
        out_specs=pl.BlockSpec(memory_space=pltpu.HBM),
        scratch_shapes=[
            pltpu.VMEM((16 * 60, 128), F32),
            pltpu.VMEM((3, 16, 32, NPHI), BF),
            pltpu.SemaphoreType.DMA((3,)),
        ],
        compiler_params=pltpu.CompilerParams(vmem_limit_bytes=6 * 2**20),
        name="to_map",
    )(got)


def paired(x):
    lead = x.shape[:-2]
    x = x.reshape(lead + (2, x.shape[-1] // 128, 128))
    return jnp.swapaxes(x, -3, -2).reshape(lead + (-1, 128))


def rowwise(x):
    return with_layout_constraint(x, Layout(major_to_minor=tuple(range(x.ndim))))


def shards(sky_coefficients, beam_window, legendre, azimuth_modes, orientation):
    me = lax.axis_index("beam").astype(jnp.int32)[None]
    def stay(x):
        return pltpu.with_memory_space_constraint(x, pltpu.HBM)

    own = stay(paired(beam_window))
    legendre = stay(legendre)
    window = lax.all_to_all(jnp.broadcast_to(rowwise(paired(beam_window))[None], (8,) + own.shape), "beam", 0, 0, tiled=True)
    coef, *rest = begin(
        me, stay(azimuth_modes), stay(paired(sky_coefficients)), stay(orientation.reshape(256, 512)), own, legendre
    )
    sent = synth(me, azimuth_modes, stay(coef), window, legendre, *rest)
    got = lax.all_to_all(sent, "blk", 0, 0, tiled=True)
    return to_map(got)


def solution(mesh):
    placed = (
        P(None, None, None, None, "blk", None),
        P(None, "beam", None),
        P("blk", None, None, None),
        P("blk"),
        P("beam", None, None),
    )
    return jax.shard_map(
        shards, mesh=mesh, in_specs=placed, out_specs=P("beam", None, "blk", None), check_vma=False
    )
```

```python
import math

import jax
import jax.numpy as jnp
from jax import lax
from jax.experimental import pallas as pl
from jax.experimental.layout import Layout, with_layout_constraint
from jax.experimental.pallas import tpu as pltpu
from jax.sharding import PartitionSpec as P

LMAX = 8192
NPHI = 128
CHUNK = 1024
TILES = CHUNK // 128
SHIFT = CHUNK.bit_length()
BF = jnp.bfloat16
F32 = jnp.float32


def mirror():
    lane = lax.broadcasted_iota(jnp.int32, (256, 256), 0)
    return jnp.where(lane + lax.broadcasted_iota(jnp.int32, (256, 256), 1) == 255, 1.0, 0.0).astype(BF)


def chunk_at(c):
    return pl.ds(pl.multiple_of(c * CHUNK, CHUNK), CHUNK)


def first_chunk(modes, slot, p, chunks):
    return jnp.minimum((modes[slot] + (1 - p)) >> SHIFT, chunks - 1)


def weighted(lines, win, bases, tiles):
    parts = []
    for base in bases:
        gain = [jnp.broadcast_to(win[pl.ds(base + 2 * i, 1), :], (16, 128)).astype(BF) for i in range(tiles)]
        gain = jnp.concatenate(gain, 1)
        parts += [line * gain for line in lines]
    return jnp.concatenate(parts, 0)


def sky_lines(coef, slot, p, tile, tiles):
    return [
        jnp.concatenate([coef[slot, p, j // 2, tile + i, pl.ds(j % 2 * 16, 16), :] for i in range(tiles)], 1)
        for j in range(6)
    ]


def orient(start, spins, acc, components, mixed):
    north, south = [None] * 12, [None] * 12
    for h in range(2):
        n = [None if start is None else start[0, pl.ds(cr * 16 + h * 8, 8), :] for cr in range(6)]
        s = [None if start is None else start[1, pl.ds(cr * 16 + h * 8, 8), :] for cr in range(6)]
        for at, k in enumerate(components):
            spin = spins[k, pl.ds(h * 8, 8), :]
            for cr in range(6):
                rows = pl.ds(at * 96 + cr * 16 + h * 8, 8)
                up, down = acc[0, rows, :], acc[1, rows, :]
                if not mixed:
                    up, down = up + down, up - down
                up, down = up * spin[:, :256], down * spin[:, 256:]
                n[cr] = up if n[cr] is None else n[cr] + up
                s[cr] = down if s[cr] is None else s[cr] + down
        for cr in range(6):
            north[2 * cr + h] = n[cr]
            south[2 * cr + h] = s[cr]
    return jnp.concatenate(north, 0), jnp.concatenate(south, 0)


def begin_kernel(
    me, modes_in, sky, orient_in, window, table, coef_out, weights, tail, partial, lead_coef, lead_leg,
    modes, raw, turns, own, win, leg, acc, wide, lines, coef, sems, leg_sems, sky_sems, coef_sems, lead_sems,
):
    mine = me[0]
    chunks = table.shape[2] // CHUNK
    rows = sky.shape[4]
    pitch = 2 * rows + 4
    fetch_modes = pltpu.make_async_copy(modes_in, modes, sems.at[0])
    fetch_orient = pltpu.make_async_copy(orient_in, turns, sems.at[1])
    fetch_window = pltpu.make_async_copy(window, own, sems.at[2])
    fetch_modes.start()

    def sky_copy(p, c):
        return pltpu.make_async_copy(sky.at[p, pl.ds(mine * 16, 16), c], raw.at[p, c], sky_sems.at[p, c])

    fetch_orient.start()
    for p in range(2):
        for c in range(3):
            sky_copy(p, c).start()
    fetch_window.start()
    fetch_modes.wait()

    def leg_copy(slot, p, c):
        at = chunk_at(c)
        return pltpu.make_async_copy(table.at[slot, p, at, :], leg.at[slot, p, at, :], leg_sems.at[slot, p, c])

    for slot in range(2):
        for p in range(2):
            lax.fori_loop(
                first_chunk(modes, slot, p, chunks), chunks, lambda c, _: (leg_copy(slot, p, c).start(), 0)[1], 0
            )

    row = lax.broadcasted_iota(jnp.int32, (8, 128), 0)
    mode = jnp.where(row < 4, modes[0], modes[1])
    column = lax.broadcasted_iota(jnp.int32, (8, 128), 1)
    phase = ((mode * column) % (2 * LMAX)).astype(F32) * (math.pi / LMAX)
    weight = jnp.where(mode == 0, 1.0, 2.0)
    basis = jnp.where(row % 4 < 2, weight * jnp.cos(phase), -weight * jnp.sin(phase))
    high = basis.astype(BF).astype(F32)
    tail[...] = jnp.where(row % 2 == 0, high, basis - high).astype(BF)

    fetch_orient.wait()
    flip = mirror()
    for t in range(4):
        for s in range(16):
            lines[pl.ds(320 * t + 20 * s, 16), :] = turns[pl.ds(16 * s, 16), pl.ds(128 * t, 128)]

    def pick(k, t):
        return lines[pl.ds(320 * t + k, 16, stride=20), :]

    for k in range(16):
        weights[k, :, pl.ds(0, 256)] = jnp.concatenate([pick(k, 0), pick(k, 1)], 1)
    south = jnp.concatenate([jnp.concatenate([pick(k, 2), pick(k, 3)], 1) for k in range(16)], 0)
    total = jnp.zeros((256, 256), F32)
    for _ in range(3):
        piece = south.astype(BF)
        total = total + jnp.dot(piece, flip, preferred_element_type=F32)
        south = south - piece.astype(F32)
    weights[:, :, pl.ds(256, 256)] = total.reshape(16, 16, 256)

    def coef_copy(m, p, c):
        return pltpu.make_async_copy(coef.at[m, p, c], coef_out.at[m, p, c], coef_sems.at[m, p, c])

    def arrange(p, c):
        sky_copy(p, c).wait()
        for s in range(16):
            wide[pl.ds(s * pitch, 2 * rows), :] = raw[p, c, s].reshape(2 * rows, 128).astype(F32)
        for r in range(2):
            for row in range(rows):
                line = wide[pl.ds(r * rows + row, 16, stride=pitch), :].astype(BF)
                coef[row % 2, p, c, row // 2, pl.ds(r * 16, 16), :] = line
        for m in range(2):
            coef_copy(m, p, c).start()

    for p in range(2):
        for c in range(3):
            arrange(p, c)

    def lead_copies():
        c = first_chunk(modes, 0, 0, chunks)
        its = pl.ds(pl.multiple_of(c * TILES, TILES), TILES)
        return (
            pltpu.make_async_copy(coef.at[0, 0, :, its], lead_coef, lead_sems.at[0]),
            pltpu.make_async_copy(leg.at[0, 0, chunk_at(c), :], lead_leg, lead_sems.at[1]),
        )

    fetch_window.wait()
    win[...] = own[...].astype(F32).reshape(win.shape)
    for slot in range(2):
        for p in range(2):

            def body(c, _, slot=slot, p=p):
                leg_copy(slot, p, c).wait()
                base = p * (2 * TILES * chunks) + c * (2 * TILES)
                tile = pl.multiple_of(c * TILES, TILES)
                lhs = weighted(sky_lines(coef, slot, p, tile, TILES), win, [base, base + 1], TILES)
                part = jnp.dot(lhs, leg[slot, p, chunk_at(c), :], preferred_element_type=F32)
                acc[p] = jnp.where(c == first_chunk(modes, slot, p, chunks), 0.0, acc[p]) + part
                return 0

            lax.fori_loop(first_chunk(modes, slot, p, chunks), chunks, body, 0)
        if slot == 0:
            for copy in lead_copies():
                copy.start()
        partial[slot, 0], partial[slot, 1] = orient(None, weights, acc, [2 * mine, 2 * mine + 1], False)
    for copy in lead_copies():
        copy.wait()
    for m in range(2):
        for p in range(2):
            for c in range(3):
                coef_copy(m, p, c).wait()


def begin(me, modes, sky, orient, window, table):
    half = table.shape[2]
    tiles = half // 128
    vm = pl.BlockSpec(memory_space=pltpu.VMEM)
    hbm = pl.BlockSpec(memory_space=pltpu.HBM)
    return pl.pallas_call(
        begin_kernel,
        out_shape=(
            pltpu.HBM((2, 2, 3, tiles, 32, 128), BF),
            jax.ShapeDtypeStruct((16, 16, 512), F32),
            jax.ShapeDtypeStruct((8, 128), BF),
            jax.ShapeDtypeStruct((2, 2, 96, 256), F32),
            jax.ShapeDtypeStruct((3, TILES, 32, 128), BF),
            jax.ShapeDtypeStruct((CHUNK, 256), BF),
        ),
        in_specs=[pl.BlockSpec(memory_space=pltpu.SMEM), hbm, hbm, hbm, hbm, hbm],
        out_specs=(hbm, vm, vm, vm, vm, vm),
        scratch_shapes=[
            pltpu.SMEM((2,), jnp.int32),
            pltpu.VMEM((2, 3, 16, 2, 2 * tiles, 128), BF),
            pltpu.VMEM((256, 512), F32),
            pltpu.VMEM(window.shape, BF),
            pltpu.VMEM((4 * tiles, 128), F32),
            pltpu.VMEM(table.shape, BF),
            pltpu.VMEM((2, 192, 256), F32),
            pltpu.VMEM((64 * tiles + 64, 128), F32),
            pltpu.VMEM((1280, 128), F32),
            pltpu.VMEM((2, 2, 3, tiles, 32, 128), BF),
            pltpu.SemaphoreType.DMA((3,)),
            pltpu.SemaphoreType.DMA((2, 2, half // CHUNK)),
            pltpu.SemaphoreType.DMA((2, 3)),
            pltpu.SemaphoreType.DMA((2, 2, 3)),
            pltpu.SemaphoreType.DMA((2,)),
        ],
        compiler_params=pltpu.CompilerParams(vmem_limit_bytes=30 * 2**20),
        cost_estimate=pl.CostEstimate(flops=4 * 10**9, bytes_accessed=16 * 10**6, transcendentals=0),
        name="begin",
    )(me, modes, sky, orient, window, table)


def synth_kernel(
    me, modes, coef_in, window, table, weights, tail, partial, lead_coef, lead_leg,
    out, coef, leg, acc, win, maps, sems, coef_sems,
):
    mine = me[0]
    halves = table.shape[2] // CHUNK * 2
    others = [(mine + 1 + j) & 7 for j in range(7)]

    def span(slot, p):
        skip = jnp.minimum((modes[slot] + (1 - p)) >> (SHIFT - 1), halves - 1)
        return (skip + 1) >> 1, skip & 1 == 1

    def copies(slot, p, c, tile, tiles):
        at = pl.ds(pl.multiple_of(tile * 128, tiles * 128), tiles * 128)
        its = pl.ds(pl.multiple_of(tile, tiles), tiles)
        return (
            pltpu.make_async_copy(
                coef_in.at[slot, p, :, its], coef.at[slot, p, :, its], coef_sems.at[slot, p, c]
            ),
            pltpu.make_async_copy(table.at[slot, p, at, :], leg.at[slot, p, at, :], sems.at[slot, p, c]),
        )

    def whole(c):
        return c, c * TILES, TILES

    def part(c):
        return c - 1, c * TILES - TILES // 2, TILES // 2

    def fetch(slot, p, where):
        for copy in copies(slot, p, *where):
            copy.start()

    def lead(at, c, tile, tiles):
        to = pl.ds(pl.multiple_of(tile * 128, tiles * 128), tiles * 128)
        its = pl.ds(pl.multiple_of(tile, tiles), tiles)
        return (
            pltpu.make_async_copy(lead_coef.at[:, pl.ds(at, tiles)], coef.at[0, 0, :, its], coef_sems.at[0, 0, c]),
            pltpu.make_async_copy(lead_leg.at[pl.ds(at * 128, tiles * 128)], leg.at[0, 0, to, :], sems.at[0, 0, c]),
        )

    def fetch_lead(at, where):
        for copy in lead(at, *where):
            copy.start()

    for slot in range(2):
        for p in range(2):
            start, half = span(slot, p)
            rest = start
            if slot == 0 and p == 0:

                @pl.when(half)
                def _(start=start):
                    fetch_lead(TILES // 2, part(start))

                @pl.when(jnp.logical_not(half))
                def _(start=start):
                    fetch_lead(0, whole(start))

                rest = jnp.where(half, start, start + 1)
            else:

                @pl.when(half)
                def _(slot=slot, p=p, start=start):
                    fetch(slot, p, part(start))

            lax.fori_loop(rest, halves // 2, lambda c, _: (fetch(slot, p, whole(c)), 0)[1], 0)
    win[...] = window[...].astype(F32).reshape(win.shape)

    def step(slot, p, c, tile, tiles):
        for copy in copies(slot, p, c, tile, tiles):
            copy.wait()
        tile = pl.multiple_of(tile, tiles)
        at = pl.ds(pl.multiple_of(tile * 128, tiles * 128), tiles * 128)
        bases = [(src * 2 + p) * (halves * TILES) + 2 * tile + kk for src in others for kk in range(2)]
        lhs = weighted(sky_lines(coef, slot, p, tile, tiles), win, bases, tiles)
        return jnp.dot(lhs, leg[slot, p, at, :], preferred_element_type=F32)

    for dst in range(16):
        out[dst, pl.ds(48, 8), :] = tail[...]
    for slot in range(2):
        for p in range(2):
            start, half = span(slot, p)

            if p == 0:

                @pl.when(half)
                def _(slot=slot, start=start):
                    acc[slot, 0] = step(slot, 0, *part(start))

                fresh = jnp.where(half, -1, start)

                def body(c, _, slot=slot, fresh=fresh):
                    more = step(slot, 0, *whole(c))
                    acc[slot, 0] = jnp.where(c == fresh, 0.0, acc[slot, 0]) + more
                    return 0

                lax.fori_loop(start, halves // 2, body, 0)
            else:

                @pl.when(half)
                def _(slot=slot, start=start):
                    more = step(slot, 1, *part(start))
                    both = acc[slot, 0]
                    acc[slot, 0] = both + more
                    acc[slot, 1] = both - more

                fresh = jnp.where(half, -1, start)

                def body(c, _, slot=slot, fresh=fresh):
                    more = step(slot, 1, *whole(c))
                    total = acc[slot, 0]
                    acc[slot, 1] = jnp.where(c == fresh, total, acc[slot, 1]) - more
                    acc[slot, 0] = total + more
                    return 0

                lax.fori_loop(start, halves // 2, body, 0)

    flip = mirror()
    group = lax.broadcasted_iota(jnp.int32, (24, 128), 1) // 32
    components = [2 * src + kk for src in others for kk in range(2)]
    for slot in range(2):
        sign = jnp.where(modes[slot] % 2 == 0, 1.0, -1.0).astype(F32)
        north, south = orient(partial.at[slot], weights, acc.at[slot], components, True)
        south = jnp.dot((south * sign).astype(BF), flip, preferred_element_type=F32)
        for tile in range(4):
            hemisphere = north if tile < 2 else south
            maps[slot, tile] = hemisphere[:, tile % 2 * 128:tile % 2 * 128 + 128]
    for slot in range(2):
        for tile in range(4):
            pieces = [maps[slot, tile, pl.ds(b, 24, stride=4), :] for b in range(4)]
            for g in range(4):
                send = pieces[g]
                for b in range(4):
                    if b != g:
                        send = jnp.where(group == b, pltpu.roll(pieces[b], ((b - g) * 32) % 128, 1), send)
                out[tile * 4 + g, pl.ds(slot * 24, 24), :] = send.astype(BF)


def synth(me, modes, coef, window, table, *rest):
    half = table.shape[2]
    vm = pl.BlockSpec(memory_space=pltpu.VMEM)
    smem = pl.BlockSpec(memory_space=pltpu.SMEM)
    hbm = pl.BlockSpec(memory_space=pltpu.HBM)
    return pl.pallas_call(
        synth_kernel,
        out_shape=jax.ShapeDtypeStruct((16, 56, 128), BF),
        in_specs=[smem, smem, hbm, vm, hbm, vm, vm, vm, vm, vm],
        out_specs=vm,
        scratch_shapes=[
            pltpu.VMEM(coef.shape, BF),
            pltpu.VMEM(table.shape, BF),
            pltpu.VMEM((2, 2, 1344, 256), F32),
            pltpu.VMEM((window.shape[0] * half // 32, 128), F32),
            pltpu.VMEM((2, 4, 96, 128), F32),
            pltpu.SemaphoreType.DMA((2, 2, half // CHUNK)),
            pltpu.SemaphoreType.DMA((2, 2, half // CHUNK)),
        ],
        compiler_params=pltpu.CompilerParams(vmem_limit_bytes=26 * 2**20),
        cost_estimate=pl.CostEstimate(flops=12 * 10**9, bytes_accessed=12 * 10**6, transcendentals=0),
        name="synth",
    )(me, modes, coef, window, table, *rest)


def map_kernel(got, out, wide, held, sems):
    for src in range(16):
        wide[pl.ds(src * 60, 56), :] = got[src].astype(F32)

    def take(row):
        return wide[pl.ds(row, 16, stride=60), :]

    basis = [take(48 + slot * 4 + r * 2 + part) for part in range(2) for r in range(2) for slot in range(2)]
    basis = jnp.concatenate(basis, 0).astype(BF)
    for c in range(3):
        for a in range(4):
            x = jnp.concatenate([take(slot * 24 + c * 8 + r * 4 + a) for r in range(2) for slot in range(2)], 0)
            x = x.T.astype(BF)
            y = jnp.dot(jnp.concatenate([x, x], 1), basis, preferred_element_type=F32)
            for b in range(4):
                held[c, 4 * a + b] = y[b * 32:(b + 1) * 32].astype(BF)
        pltpu.make_async_copy(held.at[c], out.at[:, c], sems.at[c]).start()
    for c in range(3):
        pltpu.make_async_copy(held.at[c], out.at[:, c], sems.at[c]).wait()


def to_map(got):
    vm = pl.BlockSpec(memory_space=pltpu.VMEM)
    return pl.pallas_call(
        map_kernel,
        out_shape=pltpu.HBM((16, 3, 32, NPHI), BF),
        in_specs=[vm],
        out_specs=pl.BlockSpec(memory_space=pltpu.HBM),
        scratch_shapes=[
            pltpu.VMEM((16 * 60, 128), F32),
            pltpu.VMEM((3, 16, 32, NPHI), BF),
            pltpu.SemaphoreType.DMA((3,)),
        ],
        compiler_params=pltpu.CompilerParams(vmem_limit_bytes=6 * 2**20),
        name="to_map",
    )(got)


def paired(x):
    lead = x.shape[:-2]
    x = x.reshape(lead + (2, x.shape[-1] // 128, 128))
    return jnp.swapaxes(x, -3, -2).reshape(lead + (-1, 128))


def rowwise(x):
    return with_layout_constraint(x, Layout(major_to_minor=tuple(range(x.ndim))))


def shards(sky_coefficients, beam_window, legendre, azimuth_modes, orientation):
    me = lax.axis_index("beam").astype(jnp.int32)[None]
    def stay(x):
        return pltpu.with_memory_space_constraint(x, pltpu.HBM)

    own = stay(paired(beam_window))
    legendre = stay(legendre)
    window = lax.all_to_all(jnp.broadcast_to(rowwise(paired(beam_window))[None], (8,) + own.shape), "beam", 0, 0, tiled=True)
    coef, *rest = begin(
        me, stay(azimuth_modes), stay(paired(sky_coefficients)), stay(orientation.reshape(256, 512)), own, legendre
    )
    sent = synth(me, azimuth_modes, stay(coef), window, legendre, *rest)
    got = lax.all_to_all(sent, "blk", 0, 0, tiled=True)
    return to_map(got)


def solution(mesh):
    placed = (
        P(None, None, None, None, "blk", None),
        P(None, "beam", None),
        P("blk", None, None, None),
        P("blk"),
        P("beam", None, None),
    )
    return jax.shard_map(
        shards, mesh=mesh, in_specs=placed, out_specs=P("beam", None, "blk", None), check_vma=False
    )
```

```python
import math

import jax
import jax.numpy as jnp
from jax import lax
from jax.experimental import pallas as pl
from jax.experimental.layout import Layout, with_layout_constraint
from jax.experimental.pallas import tpu as pltpu
from jax.sharding import PartitionSpec as P

LMAX = 8192
NPHI = 128
CHUNK = 1024
TILES = CHUNK // 128
SHIFT = CHUNK.bit_length()
BF = jnp.bfloat16
F32 = jnp.float32


def mirror():
    lane = lax.broadcasted_iota(jnp.int32, (256, 256), 0)
    return jnp.where(lane + lax.broadcasted_iota(jnp.int32, (256, 256), 1) == 255, 1.0, 0.0).astype(BF)


def chunk_at(c):
    return pl.ds(pl.multiple_of(c * CHUNK, CHUNK), CHUNK)


def first_chunk(modes, slot, p, chunks):
    return jnp.minimum((modes[slot] + (1 - p)) >> SHIFT, chunks - 1)


def weighted(lines, win, bases, tiles):
    parts = []
    for base in bases:
        gain = [jnp.broadcast_to(win[pl.ds(base + 2 * i, 1), :], (16, 128)).astype(BF) for i in range(tiles)]
        gain = jnp.concatenate(gain, 1)
        parts += [line * gain for line in lines]
    return jnp.concatenate(parts, 0)


def sky_lines(coef, slot, p, tile, tiles):
    return [
        jnp.concatenate([coef[slot, p, j // 2, tile + i, pl.ds(j % 2 * 16, 16), :] for i in range(tiles)], 1)
        for j in range(6)
    ]


def orient(start, spins, acc, components, mixed):
    north, south = [None] * 12, [None] * 12
    for h in range(2):
        n = [None if start is None else start[0, pl.ds(cr * 16 + h * 8, 8), :] for cr in range(6)]
        s = [None if start is None else start[1, pl.ds(cr * 16 + h * 8, 8), :] for cr in range(6)]
        for at, k in enumerate(components):
            spin = spins[k, pl.ds(h * 8, 8), :]
            for cr in range(6):
                rows = pl.ds(at * 96 + cr * 16 + h * 8, 8)
                up, down = acc[0, rows, :], acc[1, rows, :]
                if not mixed:
                    up, down = up + down, up - down
                up, down = up * spin[:, :256], down * spin[:, 256:]
                n[cr] = up if n[cr] is None else n[cr] + up
                s[cr] = down if s[cr] is None else s[cr] + down
        for cr in range(6):
            north[2 * cr + h] = n[cr]
            south[2 * cr + h] = s[cr]
    return jnp.concatenate(north, 0), jnp.concatenate(south, 0)


def begin_kernel(
    me, modes_in, sky, orient_in, window, table, coef_out, weights, tail, partial, lead_coef, lead_leg,
    modes, raw, turns, own, win, leg, acc, wide, lines, coef, sems, leg_sems, sky_sems, coef_sems, lead_sems,
):
    mine = me[0]
    chunks = table.shape[2] // CHUNK
    rows = sky.shape[4]
    pitch = 2 * rows + 4
    fetch_modes = pltpu.make_async_copy(modes_in, modes, sems.at[0])
    fetch_orient = pltpu.make_async_copy(orient_in, turns, sems.at[1])
    fetch_window = pltpu.make_async_copy(window, own, sems.at[2])
    fetch_modes.start()

    def sky_copy(p, c):
        return pltpu.make_async_copy(sky.at[p, pl.ds(mine * 16, 16), c], raw.at[p, c], sky_sems.at[p, c])

    fetch_orient.start()
    for p in range(2):
        for c in range(3):
            sky_copy(p, c).start()
    fetch_window.start()
    fetch_modes.wait()

    def leg_copy(slot, p, c):
        at = chunk_at(c)
        return pltpu.make_async_copy(table.at[slot, p, at, :], leg.at[slot, p, at, :], leg_sems.at[slot, p, c])

    for slot in range(2):
        for p in range(2):
            lax.fori_loop(
                first_chunk(modes, slot, p, chunks), chunks, lambda c, _: (leg_copy(slot, p, c).start(), 0)[1], 0
            )

    row = lax.broadcasted_iota(jnp.int32, (8, 128), 0)
    mode = jnp.where(row < 4, modes[0], modes[1])
    column = lax.broadcasted_iota(jnp.int32, (8, 128), 1)
    phase = ((mode * column) % (2 * LMAX)).astype(F32) * (math.pi / LMAX)
    weight = jnp.where(mode == 0, 1.0, 2.0)
    basis = jnp.where(row % 4 < 2, weight * jnp.cos(phase), -weight * jnp.sin(phase))
    high = basis.astype(BF).astype(F32)
    tail[...] = jnp.where(row % 2 == 0, high, basis - high).astype(BF)

    fetch_orient.wait()
    flip = mirror()
    for t in range(4):
        for s in range(16):
            lines[pl.ds(320 * t + 20 * s, 16), :] = turns[pl.ds(16 * s, 16), pl.ds(128 * t, 128)]

    def pick(k, t):
        return lines[pl.ds(320 * t + k, 16, stride=20), :]

    for k in range(16):
        weights[k, :, pl.ds(0, 256)] = jnp.concatenate([pick(k, 0), pick(k, 1)], 1)
    south = jnp.concatenate([jnp.concatenate([pick(k, 2), pick(k, 3)], 1) for k in range(16)], 0)
    total = jnp.zeros((256, 256), F32)
    for _ in range(3):
        piece = south.astype(BF)
        total = total + jnp.dot(piece, flip, preferred_element_type=F32)
        south = south - piece.astype(F32)
    weights[:, :, pl.ds(256, 256)] = total.reshape(16, 16, 256)

    def coef_copy(m, p, c):
        return pltpu.make_async_copy(coef.at[m, p, c], coef_out.at[m, p, c], coef_sems.at[m, p, c])

    def arrange(p, c):
        sky_copy(p, c).wait()
        for s in range(16):
            wide[pl.ds(s * pitch, 2 * rows), :] = raw[p, c, s].reshape(2 * rows, 128).astype(F32)
        for r in range(2):
            for row in range(rows):
                line = wide[pl.ds(r * rows + row, 16, stride=pitch), :].astype(BF)
                coef[row % 2, p, c, row // 2, pl.ds(r * 16, 16), :] = line
        for m in range(2):
            coef_copy(m, p, c).start()

    for p in range(2):
        for c in range(3):
            arrange(p, c)

    def lead_copies():
        c = first_chunk(modes, 0, 0, chunks)
        its = pl.ds(pl.multiple_of(c * TILES, TILES), TILES)
        return (
            pltpu.make_async_copy(coef.at[0, 0, :, its], lead_coef, lead_sems.at[0]),
            pltpu.make_async_copy(leg.at[0, 0, chunk_at(c), :], lead_leg, lead_sems.at[1]),
        )

    fetch_window.wait()
    win[...] = own[...].astype(F32).reshape(win.shape)
    for slot in range(2):
        for p in range(2):

            def body(c, _, slot=slot, p=p):
                leg_copy(slot, p, c).wait()
                base = p * (2 * TILES * chunks) + c * (2 * TILES)
                tile = pl.multiple_of(c * TILES, TILES)
                lhs = weighted(sky_lines(coef, slot, p, tile, TILES), win, [base, base + 1], TILES)
                part = jnp.dot(lhs, leg[slot, p, chunk_at(c), :], preferred_element_type=F32)
                acc[p] = jnp.where(c == first_chunk(modes, slot, p, chunks), 0.0, acc[p]) + part
                return 0

            lax.fori_loop(first_chunk(modes, slot, p, chunks), chunks, body, 0)
        if slot == 0:
            for copy in lead_copies():
                copy.start()
        partial[slot, 0], partial[slot, 1] = orient(None, weights, acc, [2 * mine, 2 * mine + 1], False)
    for copy in lead_copies():
        copy.wait()
    for m in range(2):
        for p in range(2):
            for c in range(3):
                coef_copy(m, p, c).wait()


def begin(me, modes, sky, orient, window, table):
    half = table.shape[2]
    tiles = half // 128
    vm = pl.BlockSpec(memory_space=pltpu.VMEM)
    hbm = pl.BlockSpec(memory_space=pltpu.HBM)
    return pl.pallas_call(
        begin_kernel,
        out_shape=(
            pltpu.HBM((2, 2, 3, tiles, 32, 128), BF),
            jax.ShapeDtypeStruct((16, 16, 512), F32),
            jax.ShapeDtypeStruct((8, 128), BF),
            jax.ShapeDtypeStruct((2, 2, 96, 256), F32),
            jax.ShapeDtypeStruct((3, TILES, 32, 128), BF),
            jax.ShapeDtypeStruct((CHUNK, 256), BF),
        ),
        in_specs=[pl.BlockSpec(memory_space=pltpu.SMEM), hbm, hbm, hbm, hbm, hbm],
        out_specs=(hbm, vm, vm, vm, vm, vm),
        scratch_shapes=[
            pltpu.SMEM((2,), jnp.int32),
            pltpu.VMEM((2, 3, 16, 2, 2 * tiles, 128), BF),
            pltpu.VMEM((256, 512), F32),
            pltpu.VMEM(window.shape, BF),
            pltpu.VMEM((4 * tiles, 128), F32),
            pltpu.VMEM(table.shape, BF),
            pltpu.VMEM((2, 192, 256), F32),
            pltpu.VMEM((64 * tiles + 64, 128), F32),
            pltpu.VMEM((1280, 128), F32),
            pltpu.VMEM((2, 2, 3, tiles, 32, 128), BF),
            pltpu.SemaphoreType.DMA((3,)),
            pltpu.SemaphoreType.DMA((2, 2, half // CHUNK)),
            pltpu.SemaphoreType.DMA((2, 3)),
            pltpu.SemaphoreType.DMA((2, 2, 3)),
            pltpu.SemaphoreType.DMA((2,)),
        ],
        compiler_params=pltpu.CompilerParams(vmem_limit_bytes=30 * 2**20),
        cost_estimate=pl.CostEstimate(flops=4 * 10**9, bytes_accessed=16 * 10**6, transcendentals=0),
        name="begin",
    )(me, modes, sky, orient, window, table)


def synth_kernel(
    me, modes, coef_in, window, table, weights, tail, partial, lead_coef, lead_leg,
    out, coef, leg, acc, win, maps, sems, coef_sems,
):
    mine = me[0]
    halves = table.shape[2] // CHUNK * 2
    others = [(mine + 1 + j) & 7 for j in range(7)]

    def span(slot, p):
        skip = jnp.minimum((modes[slot] + (1 - p)) >> (SHIFT - 1), halves - 1)
        return (skip + 1) >> 1, skip & 1 == 1

    def copies(slot, p, c, tile, tiles):
        at = pl.ds(pl.multiple_of(tile * 128, tiles * 128), tiles * 128)
        its = pl.ds(pl.multiple_of(tile, tiles), tiles)
        return (
            pltpu.make_async_copy(
                coef_in.at[slot, p, :, its], coef.at[slot, p, :, its], coef_sems.at[slot, p, c]
            ),
            pltpu.make_async_copy(table.at[slot, p, at, :], leg.at[slot, p, at, :], sems.at[slot, p, c]),
        )

    def whole(c):
        return c, c * TILES, TILES

    def part(c):
        return c - 1, c * TILES - TILES // 2, TILES // 2

    def fetch(slot, p, where):
        for copy in copies(slot, p, *where):
            copy.start()

    def lead(at, c, tile, tiles):
        to = pl.ds(pl.multiple_of(tile * 128, tiles * 128), tiles * 128)
        its = pl.ds(pl.multiple_of(tile, tiles), tiles)
        return (
            pltpu.make_async_copy(lead_coef.at[:, pl.ds(at, tiles)], coef.at[0, 0, :, its], coef_sems.at[0, 0, c]),
            pltpu.make_async_copy(lead_leg.at[pl.ds(at * 128, tiles * 128)], leg.at[0, 0, to, :], sems.at[0, 0, c]),
        )

    def fetch_lead(at, where):
        for copy in lead(at, *where):
            copy.start()

    for slot in range(2):
        for p in range(2):
            start, half = span(slot, p)
            rest = start
            if slot == 0 and p == 0:

                @pl.when(half)
                def _(start=start):
                    fetch_lead(TILES // 2, part(start))

                @pl.when(jnp.logical_not(half))
                def _(start=start):
                    fetch_lead(0, whole(start))

                rest = jnp.where(half, start, start + 1)
            else:

                @pl.when(half)
                def _(slot=slot, p=p, start=start):
                    fetch(slot, p, part(start))

            lax.fori_loop(rest, halves // 2, lambda c, _: (fetch(slot, p, whole(c)), 0)[1], 0)
    win[...] = window[...].astype(F32).reshape(win.shape)

    def step(slot, p, c, tile, tiles):
        for copy in copies(slot, p, c, tile, tiles):
            copy.wait()
        tile = pl.multiple_of(tile, tiles)
        at = pl.ds(pl.multiple_of(tile * 128, tiles * 128), tiles * 128)
        bases = [(src * 2 + p) * (halves * TILES) + 2 * tile + kk for src in others for kk in range(2)]
        lhs = weighted(sky_lines(coef, slot, p, tile, tiles), win, bases, tiles)
        return jnp.dot(lhs, leg[slot, p, at, :], preferred_element_type=F32)

    for dst in range(16):
        out[dst, pl.ds(48, 8), :] = tail[...]
    for slot in range(2):
        for p in range(2):
            start, half = span(slot, p)

            if p == 0:

                @pl.when(half)
                def _(slot=slot, start=start):
                    acc[slot, 0] = step(slot, 0, *part(start))

                fresh = jnp.where(half, -1, start)

                def body(c, _, slot=slot, fresh=fresh):
                    more = step(slot, 0, *whole(c))
                    acc[slot, 0] = jnp.where(c == fresh, 0.0, acc[slot, 0]) + more
                    return 0

                lax.fori_loop(start, halves // 2, body, 0)
            else:

                @pl.when(half)
                def _(slot=slot, start=start):
                    more = step(slot, 1, *part(start))
                    both = acc[slot, 0]
                    acc[slot, 0] = both + more
                    acc[slot, 1] = both - more

                fresh = jnp.where(half, -1, start)

                def body(c, _, slot=slot, fresh=fresh):
                    more = step(slot, 1, *whole(c))
                    total = acc[slot, 0]
                    acc[slot, 1] = jnp.where(c == fresh, total, acc[slot, 1]) - more
                    acc[slot, 0] = total + more
                    return 0

                lax.fori_loop(start, halves // 2, body, 0)

    flip = mirror()
    group = lax.broadcasted_iota(jnp.int32, (24, 128), 1) // 32
    components = [2 * src + kk for src in others for kk in range(2)]
    for slot in range(2):
        sign = jnp.where(modes[slot] % 2 == 0, 1.0, -1.0).astype(F32)
        north, south = orient(partial.at[slot], weights, acc.at[slot], components, True)
        south = jnp.dot((south * sign).astype(BF), flip, preferred_element_type=F32)
        for tile in range(4):
            hemisphere = north if tile < 2 else south
            maps[slot, tile] = hemisphere[:, tile % 2 * 128:tile % 2 * 128 + 128]
    for slot in range(2):
        for tile in range(4):
            pieces = [maps[slot, tile, pl.ds(b, 24, stride=4), :] for b in range(4)]
            for g in range(4):
                send = pieces[g]
                for b in range(4):
                    if b != g:
                        send = jnp.where(group == b, pltpu.roll(pieces[b], ((b - g) * 32) % 128, 1), send)
                out[tile * 4 + g, pl.ds(slot * 24, 24), :] = send.astype(BF)


def synth(me, modes, coef, window, table, *rest):
    half = table.shape[2]
    vm = pl.BlockSpec(memory_space=pltpu.VMEM)
    smem = pl.BlockSpec(memory_space=pltpu.SMEM)
    hbm = pl.BlockSpec(memory_space=pltpu.HBM)
    return pl.pallas_call(
        synth_kernel,
        out_shape=jax.ShapeDtypeStruct((16, 56, 128), BF),
        in_specs=[smem, smem, hbm, vm, hbm, vm, vm, vm, vm, vm],
        out_specs=vm,
        scratch_shapes=[
            pltpu.VMEM(coef.shape, BF),
            pltpu.VMEM(table.shape, BF),
            pltpu.VMEM((2, 2, 1344, 256), F32),
            pltpu.VMEM((window.shape[0] * half // 32, 128), F32),
            pltpu.VMEM((2, 4, 96, 128), F32),
            pltpu.SemaphoreType.DMA((2, 2, half // CHUNK)),
            pltpu.SemaphoreType.DMA((2, 2, half // CHUNK)),
        ],
        compiler_params=pltpu.CompilerParams(vmem_limit_bytes=26 * 2**20),
        cost_estimate=pl.CostEstimate(flops=12 * 10**9, bytes_accessed=12 * 10**6, transcendentals=0),
        name="synth",
    )(me, modes, coef, window, table, *rest)


def map_kernel(got, out, wide, held, sems):
    for src in range(16):
        wide[pl.ds(src * 60, 56), :] = got[src].astype(F32)

    def take(row):
        return wide[pl.ds(row, 16, stride=60), :]

    basis = [take(48 + slot * 4 + r * 2 + part) for part in range(2) for r in range(2) for slot in range(2)]
    basis = jnp.concatenate(basis, 0).astype(BF)
    for c in range(3):
        for a in range(4):
            x = jnp.concatenate([take(slot * 24 + c * 8 + r * 4 + a) for r in range(2) for slot in range(2)], 0)
            x = x.astype(BF)
            y = lax.dot_general(
                jnp.concatenate([x, x], 0), basis, (((0,), (0,)), ((), ())), preferred_element_type=F32
            )
            for b in range(4):
                held[c, 4 * a + b] = y[b * 32:(b + 1) * 32].astype(BF)
        pltpu.make_async_copy(held.at[c], out.at[:, c], sems.at[c]).start()
    for c in range(3):
        pltpu.make_async_copy(held.at[c], out.at[:, c], sems.at[c]).wait()


def to_map(got):
    vm = pl.BlockSpec(memory_space=pltpu.VMEM)
    return pl.pallas_call(
        map_kernel,
        out_shape=pltpu.HBM((16, 3, 32, NPHI), BF),
        in_specs=[vm],
        out_specs=pl.BlockSpec(memory_space=pltpu.HBM),
        scratch_shapes=[
            pltpu.VMEM((16 * 60, 128), F32),
            pltpu.VMEM((3, 16, 32, NPHI), BF),
            pltpu.SemaphoreType.DMA((3,)),
        ],
        compiler_params=pltpu.CompilerParams(vmem_limit_bytes=6 * 2**20),
        name="to_map",
    )(got)


def paired(x):
    lead = x.shape[:-2]
    x = x.reshape(lead + (2, x.shape[-1] // 128, 128))
    return jnp.swapaxes(x, -3, -2).reshape(lead + (-1, 128))


def rowwise(x):
    return with_layout_constraint(x, Layout(major_to_minor=tuple(range(x.ndim))))


def shards(sky_coefficients, beam_window, legendre, azimuth_modes, orientation):
    me = lax.axis_index("beam").astype(jnp.int32)[None]
    def stay(x):
        return pltpu.with_memory_space_constraint(x, pltpu.HBM)

    own = stay(paired(beam_window))
    legendre = stay(legendre)
    window = lax.all_to_all(jnp.broadcast_to(rowwise(paired(beam_window))[None], (8,) + own.shape), "beam", 0, 0, tiled=True)
    coef, *rest = begin(
        me, stay(azimuth_modes), stay(paired(sky_coefficients)), stay(orientation.reshape(256, 512)), own, legendre
    )
    sent = synth(me, azimuth_modes, stay(coef), window, legendre, *rest)
    got = lax.all_to_all(sent, "blk", 0, 0, tiled=True)
    return to_map(got)


def solution(mesh):
    placed = (
        P(None, None, None, None, "blk", None),
        P(None, "beam", None),
        P("blk", None, None, None),
        P("blk"),
        P("beam", None, None),
    )
    return jax.shard_map(
        shards, mesh=mesh, in_specs=placed, out_specs=P("beam", None, "blk", None), check_vma=False
    )
```
